256 devices in a mesh: row: 64 (over x, z, core), col: 4 (over y).
Axes of the slice: x: 4, y: 4, z: 8, core: 2. Of those that a mesh axis runs over, the one named last changes fastest.
Arguments:
- snapshots: float32 [131072, 4096], P('row', 'col'), may hold values from -1.5 to 1.5
- tests: float32 [2, 4096, 128], P(None, 'col'), may hold values from -0.09375 to 0.09375
Outputs:
- basis: float32 [131072, 256], P('row')
- coeffs: float32 [256, 4096], P(None, 'col')
The draws below stay inside these ranges and needn't reach their ends.
All inputs are finite; a program needn't handle non-finite values.
Results may differ from the reference program's by a relative error of at most 0.0003.
Values sent between devices are 32-bit elements; how exact they have to be, the bound alone decides.
A program may use at most 128 MiB of HBM per device.

```python
import math
import jax
import jax.numpy as jnp
from jax import lax

N = 4096
P_SIZE = 128
PANELS = 2
ROWS = 131072


def block_levels(stream_key, extent, pieces, low, top_value):
    factor_of = 1.0
    for dim, parts in pieces:
        steps = jax.random.uniform(jax.random.fold_in(jax.random.fold_in(stream_key, 6), dim), (parts,), jnp.float32, low / len(pieces), top_value / len(pieces))
        factor_of = factor_of * jnp.repeat(jnp.exp(steps), extent[dim] // parts).reshape((-1,) + (1,) * (len(extent) - 1 - dim))
    return factor_of


def gaussian(key, extent, spread, limit, pieces=(), held_as=jnp.bfloat16):
    array = jax.random.normal(key, extent, jnp.float32) * spread
    if len(pieces) > 0:
        array = block_levels(key, extent, pieces, -0.22, 0.18) * array
    return jnp.clip(array, min=-limit, max=limit).astype(held_as)


def setup_inputs(seed: int = 0) -> dict:
    key_list = jax.random.split(jax.random.key(seed), 3)
    snapshots = gaussian(key_list[0], (ROWS, N), 0.25, 1.5, ((0, 64), (1, 4)), jnp.float32)
    tests = gaussian(key_list[1], (PANELS, N, P_SIZE), N ** -0.5, 0.09375, ((1, 4),), jnp.float32)
    return dict(snapshots=snapshots, tests=tests)


def full_dot(left, right):
    return jnp.dot(left.astype(jnp.float32), right.astype(jnp.float32), precision=lax.Precision.HIGHEST, preferred_element_type=jnp.float32)

def left_dot(left, right):
    return lax.dot_general(left.astype(jnp.float32), right.astype(jnp.float32), (((0,), (0,)), ((), ())), precision=lax.Precision.HIGHEST, preferred_element_type=jnp.float32)

def reference(snapshots, tests):
    total = snapshots.shape[0]
    root = math.sqrt(total)
    bases = []
    coeff_list = []
    for panel in range(PANELS):
        sketch = full_dot(snapshots, tests[panel])
        if bases:
            earlier = jnp.concatenate(bases, axis=1)
            earlier_coeffs = jnp.concatenate(coeff_list, axis=0)
            small = full_dot(earlier_coeffs, tests[panel])
            sketch = sketch - full_dot(earlier, small) / root
        gram = left_dot(sketch, sketch) / total
        lower = jnp.linalg.cholesky(gram)
        inverse = jax.scipy.linalg.solve_triangular(lower, jnp.eye(gram.shape[0], dtype=jnp.float32), lower=True)
        new_basis = full_dot(sketch, inverse.T)
        bases.append(new_basis)
        coeff_list.append(left_dot(new_basis, snapshots) / root)
    return (jnp.concatenate(bases, axis=1), jnp.concatenate(coeff_list, axis=0))
```

```python
import functools
import math

import jax
import jax.numpy as jnp
from jax import lax
from jax.experimental import pallas as pl
from jax.experimental.pallas import tpu as pltpu
from jax.sharding import PartitionSpec as P

F32 = jnp.float32
BF16 = jnp.bfloat16
XS, ZS, KS, YS = 4, 8, 2, 4
MESH = pl.DeviceIdType.MESH
ROWS = 2048
COLS = 1024
CH = 256
GROUP = XS * KS


def split(value):
    high = value.astype(BF16)
    low = (value - high.astype(F32)).astype(BF16)
    return high, low


def bdot(left, right):
    return jnp.dot(left, right, preferred_element_type=F32)


def dot3(left, right):
    (lh, ll), (rh, rl) = left, right
    return bdot(lh, rh) + (bdot(ll, rh) + bdot(lh, rl))


def fdot(left, right):
    return jnp.dot(left, right, precision=lax.Precision.HIGHEST, preferred_element_type=F32)


def ds(start, size):
    return pl.ds(pl.multiple_of(start, 8), size)


def comm_kernel(
    a_hbm, t_hbm, y_out, c_out, g_out,
    abuf, tbuf, ahi, alo, th, tl, ypart, rs, yfull,
    c2, cf, ccore, cx, cz, g2, gf, gg, gz, gy,
    load_sem, rs_send, rs_recv, ag_send, ag_recv,
    core_sem, x_send, x_recv, z_send, z_recv,
    gg_send, gg_recv, gz_send, gz_recv, gy_send, gy_recv, out_sem,
):
    r = lax.axis_index("row")
    c = lax.axis_index("col")
    x, z, k = r // (ZS * KS), (r // KS) % ZS, r % KS
    g = x * KS + k

    def row_of(xx, zz, kk):
        return xx * (ZS * KS) + zz * KS + kk

    def chunk(d, s):
        return lax.rem(c + (YS - 1 - s if d == 0 else 1 + s), YS)

    def base(d, j):
        return d * (YS * CH) + j * CH

    def remote(src, dst, ssem, rsem, **where):
        return pltpu.make_async_remote_copy(
            src_ref=src, dst_ref=dst, send_sem=ssem, recv_sem=rsem,
            device_id=where, device_id_type=MESH)

    loads = {}
    t_loads = [pltpu.make_async_copy(t_hbm.at[p], tbuf.at[p], load_sem.at[8 + p]) for p in range(2)]
    for copy in t_loads:
        copy.start()
    for s in range(YS):
        for d in range(2):
            rows = ds(base(d, chunk(d, s)), CH)
            loads[s, d] = pltpu.make_async_copy(a_hbm.at[rows], abuf.at[rows], load_sem.at[2 * s + d])
            loads[s, d].start()

    barrier = pltpu.get_barrier_semaphore()
    for o in range(1, YS):
        pl.semaphore_signal(barrier, inc=1, device_id={"col": lax.rem(c + o, YS)}, device_id_type=MESH)
    for o in range(1, GROUP):
        gp = lax.rem(g + o, GROUP)
        pl.semaphore_signal(barrier, inc=1, device_id={"row": row_of(gp // KS, z, gp % KS)}, device_id_type=MESH)
    for o in range(1, ZS):
        pl.semaphore_signal(barrier, inc=1, device_id={"row": row_of(x, lax.rem(z + o, ZS), k)}, device_id_type=MESH)

    for p in range(2):
        t_loads[p].wait()
        high, low = split(tbuf[p])
        th[:, p * 128:(p + 1) * 128] = high
        tl[:, p * 128:(p + 1) * 128] = low

    nexts = (lax.rem(c + 1, YS), lax.rem(c + YS - 1, YS))
    sends = []

    def rs_copy(p, d, s):
        src = ypart.at[p, ds(base(d, chunk(d, 0)), CH)] if s == 0 else rs.at[p, d, s - 1]
        return remote(src, rs.at[p, d, s], rs_send.at[p, d, s], rs_recv.at[p, d, s], col=nexts[d])

    def ag_copy(p, d, s):
        j = lax.rem(c + (YS - s if d == 0 else s), YS)
        ref = yfull.at[p, ds(base(d, j), CH)]
        return remote(ref, ref, ag_send.at[p, d, s], ag_recv.at[p, d, s], col=nexts[d])

    def sketch(d, s):
        loads[s, d].wait()
        rows = ds(base(d, chunk(d, s)), CH)
        high, low = split(abuf[rows, :])
        ahi[rows, :] = high
        alo[rows, :] = low
        part = dot3((high, low), (th[...], tl[...]))
        ypart[0, rows, :] = part[:, :128]
        ypart[1, rows, :] = part[:, 128:]

    for d in range(2):
        sketch(d, 0)
        if d == 0:
            pl.semaphore_wait(barrier, (YS - 1) + (GROUP - 1) + (ZS - 1))
        for p in range(2):
            copy = rs_copy(p, d, 0)
            copy.start()
            sends.append(copy)
    for d in range(2):
        sketch(d, 1)
    for s in range(1, YS):
        for p in range(2):
            for d in range(2):
                rs_copy(p, d, s - 1).wait_recv()
                rows = ds(base(d, chunk(d, s)), CH)
                if s < YS - 1:
                    rs[p, d, s - 1] = rs[p, d, s - 1] + ypart[p, rows, :]
                    copy = rs_copy(p, d, s)
                else:
                    yfull[p, rows, :] = rs[p, d, s - 1] + ypart[p, rows, :]
                    copy = ag_copy(p, d, 0)
                copy.start()
                sends.append(copy)
        if s < YS - 1:
            for d in range(2):
                sketch(d, s + 1)

    own = [jnp.concatenate([yfull[0, ds(base(d, c), CH), :], yfull[1, ds(base(d, c), CH), :]], axis=1) for d in range(2)]
    own = jnp.concatenate(own, axis=0)
    gram = dot3(split(own.T), split(own))
    g2[0:256, :] = gram[:, :128]
    g2[256:512, :] = gram[:, 128:]

    def g_copy(o):
        gp = lax.rem(g + o, GROUP)
        return remote(g2.at[ds(gp * 64, 64)], gg.at[o - 1], gg_send.at[0, o - 1], gg_recv.at[0, o - 1],
                      row=row_of(gp // KS, z, gp % KS))

    def gz_copy(o):
        zp = lax.rem(z + o, ZS)
        return remote(g2.at[ds(g * 64 + zp * 8, 8)], gz.at[o - 1], gz_send.at[0, o - 1], gz_recv.at[0, o - 1],
                      row=row_of(x, zp, k))

    gmine = ds(g * 64 + z * 8, 8)

    def gy_copy(o):
        return remote(g2.at[gmine], gy.at[o - 1], gy_send.at[o - 1], gy_recv.at[o - 1], col=lax.rem(c + o, YS))

    def gz_back(o):
        zp = lax.rem(z + o, ZS)
        return remote(gf.at[gmine], gf.at[gmine], gz_send.at[1, o - 1], gz_recv.at[1, o - 1], row=row_of(x, zp, k))

    def g_back(o):
        gp = lax.rem(g + o, GROUP)
        ref = gf.at[ds(g * 64, 64)]
        return remote(ref, ref, gg_send.at[1, o - 1], gg_recv.at[1, o - 1], row=row_of(gp // KS, z, gp % KS))

    def start(make, count):
        for o in range(1, count):
            copy = make(o)
            copy.start()
            sends.append(copy)

    def arrive(make, count):
        for o in range(1, count):
            make(o).wait_recv()

    def coeffs(d, j, first):
        rows = ds(base(d, j), CH)
        both = jnp.concatenate([yfull[0, rows, :].T, yfull[1, rows, :].T], axis=0)
        left = split(both)
        for t in range(4):
            lanes = slice(t * 256, (t + 1) * 256)
            part = dot3(left, (ahi[rows, lanes], alo[rows, lanes]))
            for h in range(2):
                out = slice((2 * t + h) * 256, (2 * t + h + 1) * 256)
                if first:
                    c2[out, :] = part[:, h * 128:(h + 1) * 128]
                else:
                    c2[out, :] += part[:, h * 128:(h + 1) * 128]

    start(g_copy, GROUP)
    coeffs(0, c, True)
    coeffs(1, c, False)

    def g_stage1():
        arrive(g_copy, GROUP)
        rows = ds(g * 64, 64)
        total = g2[rows, :]
        for o in range(GROUP - 1):
            total = total + gg[o]
        g2[rows, :] = total
        start(gz_copy, ZS)

    def g_stage2():
        arrive(gz_copy, ZS)
        total = g2[gmine, :]
        for o in range(ZS - 1):
            total = total + gz[o]
        g2[gmine, :] = total
        start(gy_copy, YS)

    def g_stage3():
        arrive(gy_copy, YS)
        gf[gmine, :] = (g2[gmine, :] + gy[1]) + (gy[0] + gy[2])
        start(gz_back, ZS)

    def g_stage4():
        arrive(gz_back, ZS)
        start(g_back, GROUP)

    stages = {0: g_stage1, 1: g_stage2, 2: g_stage3}
    for s in range(YS - 1):
        for p in range(2):
            for d in range(2):
                ag_copy(p, d, s).wait_recv()
                if s < YS - 2:
                    copy = ag_copy(p, d, s + 1)
                    copy.start()
                    sends.append(copy)
        stages[s]()
        for d in range(2):
            j = lax.rem(c + (YS - 1 - s if d == 0 else 1 + s), YS)
            coeffs(d, j, False)
    y_copy = pltpu.make_async_copy(yfull, y_out, out_sem.at[0])
    y_copy.start()

    half = k * 1024
    core_peer = row_of(x, z, 1 - k)
    core_copy = remote(c2.at[ds((1 - k) * 1024, 1024)], ccore, core_sem.at[0], core_sem.at[1], row=core_peer)
    core_copy.start()
    sends.append(core_copy)
    g_stage4()
    core_copy.wait_recv()
    mine = ds(half, 1024)
    c2[mine, :] += ccore[...]

    def x_copy(o):
        xp = lax.rem(x + o, XS)
        return remote(c2.at[ds(half + xp * 256, 256)], cx.at[o - 1], x_send.at[0, o - 1], x_recv.at[0, o - 1],
                      row=row_of(xp, z, k))

    quarter = half + x * 256

    def z_copy(o):
        zp = lax.rem(z + o, ZS)
        return remote(c2.at[ds(quarter + zp * 32, 32)], cz.at[o - 1], z_send.at[0, o - 1], z_recv.at[0, o - 1],
                      row=row_of(x, zp, k))

    piece = ds(quarter + z * 32, 32)

    def z_back(o):
        return remote(cf.at[piece], cf.at[piece], z_send.at[1, o - 1], z_recv.at[1, o - 1],
                      row=row_of(x, lax.rem(z + o, ZS), k))

    def x_back(o):
        ref = cf.at[ds(quarter, 256)]
        return remote(ref, ref, x_send.at[1, o - 1], x_recv.at[1, o - 1], row=row_of(lax.rem(x + o, XS), z, k))

    start(x_copy, XS)
    arrive(x_copy, XS)
    rows = ds(quarter, 256)
    c2[rows, :] = (c2[rows, :] + cx[0]) + (cx[1] + cx[2])
    start(z_copy, ZS)
    arrive(g_back, GROUP)
    g_out_copy = pltpu.make_async_copy(gf, g_out, out_sem.at[1])
    g_out_copy.start()
    arrive(z_copy, ZS)
    total = c2[piece, :]
    for o in range(ZS - 1):
        total = total + cz[o]
    cf[piece, :] = total
    start(z_back, ZS)
    arrive(z_back, ZS)
    start(x_back, XS)
    arrive(x_back, XS)
    core_back = remote(cf.at[mine], cf.at[mine], core_sem.at[2], core_sem.at[3], row=core_peer)
    core_back.start()
    sends.append(core_back)
    core_back.wait_recv()
    c_copy = pltpu.make_async_copy(cf, c_out, out_sem.at[2])
    c_copy.start()
    for copy in sends:
        copy.wait_send()
    y_copy.wait()
    g_out_copy.wait()
    c_copy.wait()


def eliminate(work):
    row = lax.broadcasted_iota(jnp.int32, (8, 256), 0)
    for b in range(16):
        slab = work[8 * b:8 * b + 8, :]
        for i in range(8):
            column = slab[:, 8 * b + i:8 * b + i + 1]
            scale = lax.rsqrt(column[i:i + 1, :])
            line = slab[i:i + 1, :] * scale
            below = slab - (column * scale) * line
            slab = jnp.where(row > i, below, jnp.where(row == i, jnp.broadcast_to(line, (8, 256)), slab))
        work[8 * b:8 * b + 8, :] = slab
        if b < 15:
            low = 8 * b + 8
            across = slab[:, :128].T
            work[low:, :] = work[low:, :] - fdot(across[low:, :], slab)


def finish_kernel(total, y_ref, c_ref, g_ref, basis_ref, coeff_ref, work):
    inv_total = 1.0 / total
    inv_root = 1.0 / math.sqrt(total)
    eye = (lax.broadcasted_iota(jnp.int32, (128, 128), 0) == lax.broadcasted_iota(jnp.int32, (128, 128), 1)).astype(F32)
    work[:, :128] = g_ref[0:128, :] * inv_total
    work[:, 128:] = eye
    eliminate(work)
    inv0 = work[:, 128:]
    cross = fdot(inv0, g_ref[256:384, :] * inv_total)
    work[:, :128] = g_ref[384:512, :] * inv_total - fdot(cross.T, cross)
    work[:, 128:] = eye
    eliminate(work)
    inv1 = work[:, 128:]
    corner = -fdot(fdot(inv1, cross.T), inv0)
    full = jnp.concatenate(
        [jnp.concatenate([inv0, jnp.zeros_like(inv0)], axis=1), jnp.concatenate([corner, inv1], axis=1)], axis=0)
    across = split(full.T)
    left = split(full)
    for i in range(8):
        rows = slice(i * 256, (i + 1) * 256)
        y = jnp.concatenate([y_ref[0, rows, :], y_ref[1, rows, :]], axis=1)
        basis_ref[rows, :] = dot3(split(y), across)
    for t in range(8):
        coeff_ref[:, t * 128:(t + 1) * 128] = dot3(left, split(c_ref[t * 256:(t + 1) * 256, :])) * inv_root


def per_device(snapshots, tests):
    total = ROWS * XS * ZS * KS
    vmem, dma = pltpu.VMEM, pltpu.SemaphoreType.DMA
    any_spec = pl.BlockSpec(memory_space=pl.ANY)
    y, cc, gg = pl.pallas_call(
        comm_kernel,
        out_shape=(
            jax.ShapeDtypeStruct((2, ROWS, 128), F32),
            jax.ShapeDtypeStruct((2048, 128), F32),
            jax.ShapeDtypeStruct((512, 128), F32)),
        in_specs=[any_spec, any_spec],
        out_specs=(any_spec, any_spec, any_spec),
        scratch_shapes=[
            vmem((ROWS, COLS), F32), vmem((2, COLS, 128), F32), vmem((ROWS, COLS), BF16), vmem((ROWS, COLS), BF16),
            vmem((COLS, 256), BF16), vmem((COLS, 256), BF16), vmem((2, ROWS, 128), F32),
            vmem((2, 2, 3, CH, 128), F32), vmem((2, ROWS, 128), F32),
            vmem((2048, 128), F32), vmem((2048, 128), F32), vmem((1024, 128), F32), vmem((3, 256, 128), F32),
            vmem((7, 32, 128), F32), vmem((512, 128), F32), vmem((512, 128), F32), vmem((7, 64, 128), F32),
            vmem((7, 8, 128), F32), vmem((3, 8, 128), F32),
            dma((10,)), dma((2, 2, 3)), dma((2, 2, 3)), dma((2, 2, 3)), dma((2, 2, 3)),
            dma((4,)), dma((2, 3)), dma((2, 3)), dma((2, 7)), dma((2, 7)),
            dma((2, 7)), dma((2, 7)), dma((2, 7)), dma((2, 7)), dma((3,)), dma((3,)), dma((3,))],
        compiler_params=pltpu.CompilerParams(collective_id=0, has_side_effects=True, vmem_limit_bytes=56 << 20),
    )(snapshots, tests)
    return pl.pallas_call(
        functools.partial(finish_kernel, float(total)),
        out_shape=(jax.ShapeDtypeStruct((ROWS, 256), F32), jax.ShapeDtypeStruct((256, COLS), F32)),
        scratch_shapes=[vmem((128, 256), F32)],
        compiler_params=pltpu.CompilerParams(vmem_limit_bytes=40 << 20),
    )(y, cc, gg)


def solution(mesh):
    in_specs = (P("row", "col"), P(None, "col", None))
    out_specs = (P("row", None), P(None, "col"))
    return jax.shard_map(per_device, mesh=mesh, in_specs=in_specs, out_specs=out_specs, check_vma=False)
```

```python
import math

import jax
import jax.numpy as jnp
from jax import lax
from jax.experimental import pallas as pl
from jax.experimental.pallas import tpu as pltpu
from jax.sharding import PartitionSpec as P

F32 = jnp.float32
BF16 = jnp.bfloat16
XS, ZS, KS, YS = 4, 8, 2, 4
MESH = pl.DeviceIdType.MESH
ROWS = 2048
COLS = 1024
CH = 256
GROUP = XS * KS
TOTAL = float(ROWS * XS * ZS * KS)
INV_TOTAL = 1.0 / TOTAL
INV_ROOT = 1.0 / math.sqrt(TOTAL)


def split(value):
    high = value.astype(BF16)
    low = (value - high.astype(F32)).astype(BF16)
    return high, low


def bdot(left, right):
    return jnp.dot(left, right, preferred_element_type=F32)


def dot3(left, right):
    (lh, ll), (rh, rl) = left, right
    return bdot(lh, rh) + (bdot(ll, rh) + bdot(lh, rl))


def fdot(left, right):
    return jnp.dot(left, right, precision=lax.Precision.HIGHEST, preferred_element_type=F32)


def ds(start, size):
    return pl.ds(pl.multiple_of(start, 8), size)


def twice(value):
    return jnp.concatenate([value, value], axis=1)


def eliminate(work, first):
    row = lax.broadcasted_iota(jnp.int32, (8, 256), 0)
    count = 4
    slabs = [work[8 * (first + q):8 * (first + q) + 8, :] for q in range(count)]
    for q in range(count):
        off = 8 * (first + q)

        def spread(slab, j):
            return jnp.broadcast_to(slab[:, off + j:off + j + 1], (8, 128))

        columns = [spread(slabs[q], j) for j in range(8)]
        diag = [[jnp.broadcast_to(columns[j][i:i + 1, :], (8, 128)) for j in range(i + 1)] for i in range(8)]
        lines = [jnp.broadcast_to(slabs[q][i:i + 1, :], (8, 256)) for i in range(8)]
        below = {p: [spread(slabs[p], j) for j in range(8)] for p in range(q + 1, count)}
        out = None
        for j in range(8):
            scale = lax.rsqrt(diag[j][j])
            lines[j] = lines[j] * twice(scale)
            low = [None] * (j + 1) + [diag[i][j] * scale for i in range(j + 1, 8)]
            for i in range(j + 1, 8):
                for m in range(j + 1, i + 1):
                    diag[i][m] = diag[i][m] - low[i] * low[m]
                lines[i] = lines[i] - twice(low[i]) * lines[j]
            for p in range(q + 1, count):
                factor = below[p][j] * scale
                for m in range(j + 1, 8):
                    below[p][m] = below[p][m] - factor * low[m]
                slabs[p] = slabs[p] - twice(factor) * lines[j]
            out = lines[j] if out is None else jnp.where(row == j, lines[j], out)
        slabs[q] = out
        work[off:off + 8, :] = out
    end = 8 * (first + count)
    if end < 128:
        done = work[8 * first:end, :]
        work[end:, :] = work[end:, :] - fdot(done[:, :128].T[end:, :], done)


def comm_kernel(
    a_hbm, t_hbm, basis_out, coeff_out,
    abuf, tbuf, ahi, alo, th, tl, ypart, rs, yfull,
    c2, cf, ccore, cx, cz, g2, gf, gg, gz, gy, work, inv, bbuf, obuf,
    load_sem, rs_send, rs_recv, ag_send, ag_recv,
    core_send, core_recv, x_send, x_recv, z_send, z_recv,
    gg_send, gg_recv, gz_send, gz_recv, gy_send, gy_recv, out_sem,
):
    r = lax.axis_index("row")
    c = lax.axis_index("col")
    x, z, k = r // (ZS * KS), (r // KS) % ZS, r % KS
    g = x * KS + k

    def row_of(xx, zz, kk):
        return xx * (ZS * KS) + zz * KS + kk

    def chunk(d, s):
        return lax.rem(c + (YS - 1 - s if d == 0 else 1 + s), YS)

    def base(d, j):
        return d * (YS * CH) + j * CH

    def remote(src, dst, ssem, rsem, **where):
        return pltpu.make_async_remote_copy(
            src_ref=src, dst_ref=dst, send_sem=ssem, recv_sem=rsem,
            device_id=where, device_id_type=MESH)

    sends = []

    def go(copy):
        copy.start()
        sends.append(copy)

    def start(make, count):
        for o in range(1, count):
            go(make(o))

    def arrive(make, count):
        for o in range(1, count):
            make(o).wait_recv()

    loads = {}
    t_loads = [pltpu.make_async_copy(t_hbm.at[p], tbuf.at[p], load_sem.at[8 + p]) for p in range(2)]
    for copy in t_loads:
        copy.start()
    for s in range(YS):
        for d in range(2):
            rows = ds(base(d, chunk(d, s)), CH)
            loads[s, d] = pltpu.make_async_copy(a_hbm.at[rows], abuf.at[rows], load_sem.at[2 * s + d])
            loads[s, d].start()

    barrier = pltpu.get_barrier_semaphore()
    for o in range(1, YS):
        pl.semaphore_signal(barrier, inc=1, device_id={"col": lax.rem(c + o, YS)}, device_id_type=MESH)
    for o in range(1, GROUP):
        gp = lax.rem(g + o, GROUP)
        pl.semaphore_signal(barrier, inc=1, device_id={"row": row_of(gp // KS, z, gp % KS)}, device_id_type=MESH)
    for o in range(1, ZS):
        pl.semaphore_signal(barrier, inc=1, device_id={"row": row_of(x, lax.rem(z + o, ZS), k)}, device_id_type=MESH)

    for p in range(2):
        t_loads[p].wait()
        high, low = split(tbuf[p])
        th[:, p * 128:(p + 1) * 128] = high
        tl[:, p * 128:(p + 1) * 128] = low

    nexts = (lax.rem(c + 1, YS), lax.rem(c + YS - 1, YS))

    def rs_copy(p, d, s):
        src = ypart.at[p, ds(base(d, chunk(d, 0)), CH)] if s == 0 else rs.at[p, d, s - 1]
        return remote(src, rs.at[p, d, s], rs_send.at[p, d, s], rs_recv.at[p, d, s], col=nexts[d])

    def ag_copy(p, d, s, h):
        j = lax.rem(c + (YS - s if d == 0 else s), YS)
        ref = yfull.at[p, ds(base(d, j) + h * (CH // 2), CH // 2)]
        return remote(ref, ref, ag_send.at[p, d, s, h], ag_recv.at[p, d, s, h], col=nexts[d])

    def sketch(d, s):
        loads[s, d].wait()
        rows = ds(base(d, chunk(d, s)), CH)
        high, low = split(abuf[rows, :])
        ahi[rows, :] = high
        alo[rows, :] = low
        part = dot3((high, low), (th[...], tl[...]))
        ypart[0, rows, :] = part[:, :128]
        ypart[1, rows, :] = part[:, 128:]

    def g_copy(o):
        gp = lax.rem(g + o, GROUP)
        return remote(g2.at[ds(gp * 64, 64)], gg.at[o - 1], gg_send.at[0, o - 1], gg_recv.at[0, o - 1],
                      row=row_of(gp // KS, z, gp % KS))

    def gz_copy(o):
        zp = lax.rem(z + o, ZS)
        return remote(g2.at[ds(g * 64 + zp * 8, 8)], gz.at[o - 1], gz_send.at[0, o - 1], gz_recv.at[0, o - 1],
                      row=row_of(x, zp, k))

    gmine = ds(g * 64 + z * 8, 8)

    def gy_copy(o):
        return remote(g2.at[gmine], gy.at[o - 1], gy_send.at[o - 1], gy_recv.at[o - 1], col=lax.rem(c + o, YS))

    def gz_back(o):
        return remote(gf.at[gmine], gf.at[gmine], gz_send.at[1, o - 1], gz_recv.at[1, o - 1],
                      row=row_of(x, lax.rem(z + o, ZS), k))

    def g_back(o):
        gp = lax.rem(g + o, GROUP)
        ref = gf.at[ds(g * 64, 64)]
        return remote(ref, ref, gg_send.at[1, o - 1], gg_recv.at[1, o - 1], row=row_of(gp // KS, z, gp % KS))

    def gram_local():
        own = [jnp.concatenate([yfull[p, ds(base(d, c), CH), :] for p in range(2)], axis=1) for d in range(2)]
        own = jnp.concatenate(own, axis=0)
        gram = dot3(split(own.T), split(own))
        g2[0:256, :] = gram[:, :128]
        g2[256:512, :] = gram[:, 128:]
        start(g_copy, GROUP)

    def g_stage1():
        arrive(g_copy, GROUP)
        rows = ds(g * 64, 64)
        total = g2[rows, :]
        for o in range(GROUP - 1):
            total = total + gg[o]
        g2[rows, :] = total
        start(gz_copy, ZS)

    def g_stage2():
        arrive(gz_copy, ZS)
        total = g2[gmine, :]
        for o in range(ZS - 1):
            total = total + gz[o]
        g2[gmine, :] = total
        start(gy_copy, YS)

    def g_stage3():
        arrive(gy_copy, YS)
        gf[gmine, :] = (g2[gmine, :] + gy[1]) + (gy[0] + gy[2])
        start(gz_back, ZS)

    def g_stage4():
        arrive(gz_back, ZS)
        start(g_back, GROUP)

    def g_stage5():
        arrive(g_back, GROUP)

    def product(p, d, j, first):
        rows = ds(base(d, j), CH)
        left = split(yfull[p, rows, :].T)
        for t in range(4):
            lanes = slice(t * 256, (t + 1) * 256)
            part = dot3(left, (ahi[rows, lanes], alo[rows, lanes]))
            for h in range(2):
                out = slice((2 * t + h) * 128, (2 * t + h + 1) * 128)
                if first:
                    c2[p, out, :] = part[:, h * 128:(h + 1) * 128]
                else:
                    c2[p, out, :] += part[:, h * 128:(h + 1) * 128]

    def step_products(p, s):
        for d in range(2):
            product(p, d, lax.rem(c + (YS - 1 - s if d == 0 else 1 + s), YS), False)

    half = k * 512
    mine = ds(half, 512)
    quarter = half + x * 128
    piece = ds(quarter + z * 16, 16)
    core_peer = row_of(x, z, 1 - k)

    def core_copy(p):
        return remote(c2.at[p, ds((1 - k) * 512, 512)], ccore.at[p], core_send.at[p, 0], core_recv.at[p, 0],
                      row=core_peer)

    def core_back(p):
        return remote(cf.at[p, mine], cf.at[p, mine], core_send.at[p, 1], core_recv.at[p, 1], row=core_peer)

    def x_copy(p):
        def make(o):
            xp = lax.rem(x + o, XS)
            return remote(c2.at[p, ds(half + xp * 128, 128)], cx.at[p, o - 1],
                          x_send.at[p, 0, o - 1], x_recv.at[p, 0, o - 1], row=row_of(xp, z, k))
        return make

    def z_copy(p):
        def make(o):
            zp = lax.rem(z + o, ZS)
            return remote(c2.at[p, ds(quarter + zp * 16, 16)], cz.at[p, o - 1],
                          z_send.at[p, 0, o - 1], z_recv.at[p, 0, o - 1], row=row_of(x, zp, k))
        return make

    def z_back(p):
        def make(o):
            return remote(cf.at[p, piece], cf.at[p, piece], z_send.at[p, 1, o - 1], z_recv.at[p, 1, o - 1],
                          row=row_of(x, lax.rem(z + o, ZS), k))
        return make

    def x_back(p):
        def make(o):
            ref = cf.at[p, ds(quarter, 128)]
            return remote(ref, ref, x_send.at[p, 1, o - 1], x_recv.at[p, 1, o - 1],
                          row=row_of(lax.rem(x + o, XS), z, k))
        return make

    def c_stage1(p):
        core_copy(p).wait_recv()
        c2[p, mine, :] += ccore[p]
        start(x_copy(p), XS)

    def c_stage2(p):
        arrive(x_copy(p), XS)
        rows = ds(quarter, 128)
        c2[p, rows, :] = (c2[p, rows, :] + cx[p, 0]) + (cx[p, 1] + cx[p, 2])
        start(z_copy(p), ZS)

    def c_stage3(p):
        arrive(z_copy(p), ZS)
        total = c2[p, piece, :]
        for o in range(ZS - 1):
            total = total + cz[p, o]
        cf[p, piece, :] = total
        start(z_back(p), ZS)

    def c_stage4(p):
        arrive(z_back(p), ZS)
        start(x_back(p), XS)

    def c_stage5(p):
        arrive(x_back(p), XS)
        go(core_back(p))

    def c_stage6(p):
        core_back(p).wait_recv()

    def eye():
        shape = (128, 128)
        same = lax.broadcasted_iota(jnp.int32, shape, 0) == lax.broadcasted_iota(jnp.int32, shape, 1)
        return same.astype(F32)

    def factor_start0():
        work[0, :, :128] = gf[0:128, :] * INV_TOTAL
        work[0, :, 128:] = eye()

    def factor_start1():
        cross = fdot(work[0, :, 128:], gf[256:384, :] * INV_TOTAL)
        work[1, :, :128] = gf[384:512, :] * INV_TOTAL - fdot(cross.T, cross)
        work[1, :, 128:] = eye()
        inv[:128, 128:] = cross

    def factor_end():
        inv0, inv1 = work[0, :, 128:], work[1, :, 128:]
        corner = -fdot(fdot(inv1, inv[:128, 128:].T), inv0)
        inv[:128, :128] = inv0
        inv[:128, 128:] = jnp.zeros_like(inv0)
        inv[128:, :128] = corner
        inv[128:, 128:] = inv1

    def gathered(p):
        return jnp.concatenate([cf[p, t * 128:(t + 1) * 128, :] for t in range(8)], axis=1)

    basis_copies = []

    def bases():
        across = split(inv[...].T)
        for i in range(8):
            rows = slice(i * CH, (i + 1) * CH)
            y = jnp.concatenate([yfull[0, rows, :], yfull[1, rows, :]], axis=1)
            bbuf[rows, :] = dot3(split(y), across)
            copy = pltpu.make_async_copy(bbuf.at[rows], basis_out.at[rows], out_sem.at[i])
            copy.start()
            basis_copies.append(copy)

    def ag_pass(p, s, h):
        for d in range(2):
            ag_copy(p, d, s, h).wait_recv()
            if s < YS - 2:
                go(ag_copy(p, d, s + 1, h))

    for d in range(2):
        sketch(d, 0)
        if d == 0:
            pl.semaphore_wait(barrier, (YS - 1) + (GROUP - 1) + (ZS - 1))
        for p in range(2):
            go(rs_copy(p, d, 0))
    for d in range(2):
        sketch(d, 1)
    for s in range(1, YS):
        for p in range(2):
            for d in range(2):
                rs_copy(p, d, s - 1).wait_recv()
                rows = ds(base(d, chunk(d, s)), CH)
                if s < YS - 1:
                    rs[p, d, s - 1] = rs[p, d, s - 1] + ypart[p, rows, :]
                    go(rs_copy(p, d, s))
                else:
                    yfull[p, rows, :] = rs[p, d, s - 1] + ypart[p, rows, :]
                    if p == 0:
                        for h in range(2):
                            go(ag_copy(0, d, 0, h))
        if s < YS - 1:
            for d in range(2):
                sketch(d, s + 1)

    gram_local()
    product(0, 0, c, True)
    product(0, 1, c, False)
    ag_pass(0, 0, 0)
    g_stage1()
    ag_pass(0, 0, 1)
    g_stage2()
    step_products(0, 0)
    ag_pass(0, 1, 0)
    g_stage3()
    ag_pass(0, 1, 1)
    for h in range(2):
        for d in range(2):
            go(ag_copy(1, d, 0, h))
    step_products(0, 1)
    g_stage4()
    ag_pass(0, 2, 0)
    ag_pass(0, 2, 1)
    step_products(0, 2)
    go(core_copy(0))
    g_stage5()
    factor_start0()
    eliminate(work.at[0], 0)
    c_stage1(0)
    ag_pass(1, 0, 0)
    product(1, 0, c, True)
    product(1, 1, c, False)
    ag_pass(1, 0, 1)
    eliminate(work.at[0], 4)
    eliminate(work.at[0], 8)
    step_products(1, 0)
    ag_pass(1, 1, 0)
    c_stage2(0)
    eliminate(work.at[0], 12)
    ag_pass(1, 1, 1)
    factor_start1()
    eliminate(work.at[1], 0)
    c_stage3(0)
    step_products(1, 1)
    ag_pass(1, 2, 0)
    ag_pass(1, 2, 1)
    step_products(1, 2)
    go(core_copy(1))
    c_stage4(0)
    eliminate(work.at[1], 4)
    c_stage1(1)
    eliminate(work.at[1], 8)
    eliminate(work.at[1], 12)
    c_stage5(0)
    c_stage2(1)
    factor_end()
    c_stage6(0)
    first = dot3(split(inv[:, :128]), split(gathered(0)))
    obuf[:128, :] = first[:128, :] * INV_ROOT
    obuf[128:, :] = first[128:, :]
    coeff_copy0 = pltpu.make_async_copy(obuf.at[0:128], coeff_out.at[0:128], out_sem.at[8])
    coeff_copy0.start()
    c_stage3(1)
    bases()
    c_stage4(1)
    c_stage5(1)
    c_stage6(1)
    last = dot3(split(inv[128:, 128:]), split(gathered(1)))
    obuf[128:, :] = (obuf[128:, :] + last) * INV_ROOT
    coeff_copy1 = pltpu.make_async_copy(obuf.at[128:256], coeff_out.at[128:256], out_sem.at[9])
    coeff_copy1.start()
    for copy in sends:
        copy.wait_send()
    for copy in basis_copies:
        copy.wait()
    coeff_copy0.wait()
    coeff_copy1.wait()


def per_device(snapshots, tests):
    vmem, dma = pltpu.VMEM, pltpu.SemaphoreType.DMA
    any_spec = pl.BlockSpec(memory_space=pl.ANY)
    return pl.pallas_call(
        comm_kernel,
        out_shape=(jax.ShapeDtypeStruct((ROWS, 256), F32), jax.ShapeDtypeStruct((256, COLS), F32)),
        in_specs=[any_spec, any_spec],
        out_specs=(any_spec, any_spec),
        scratch_shapes=[
            vmem((ROWS, COLS), F32), vmem((2, COLS, 128), F32), vmem((ROWS, COLS), BF16), vmem((ROWS, COLS), BF16),
            vmem((COLS, 256), BF16), vmem((COLS, 256), BF16), vmem((2, ROWS, 128), F32),
            vmem((2, 2, 3, CH, 128), F32), vmem((2, ROWS, 128), F32),
            vmem((2, 1024, 128), F32), vmem((2, 1024, 128), F32), vmem((2, 512, 128), F32),
            vmem((2, 3, 128, 128), F32), vmem((2, 7, 16, 128), F32),
            vmem((512, 128), F32), vmem((512, 128), F32), vmem((7, 64, 128), F32),
            vmem((7, 8, 128), F32), vmem((3, 8, 128), F32), vmem((2, 128, 256), F32), vmem((256, 256), F32),
            vmem((ROWS, 256), F32), vmem((256, COLS), F32),
            dma((10,)), dma((2, 2, 3)), dma((2, 2, 3)), dma((2, 2, 3, 2)), dma((2, 2, 3, 2)),
            dma((2, 2)), dma((2, 2)), dma((2, 2, 3)), dma((2, 2, 3)), dma((2, 2, 7)), dma((2, 2, 7)),
            dma((2, 7)), dma((2, 7)), dma((2, 7)), dma((2, 7)), dma((3,)), dma((3,)), dma((10,))],
        compiler_params=pltpu.CompilerParams(collective_id=0, has_side_effects=True, vmem_limit_bytes=56 << 20),
    )(snapshots, tests)


def solution(mesh):
    in_specs = (P("row", "col"), P(None, "col", None))
    out_specs = (P("row", None), P(None, "col"))
    return jax.shard_map(per_device, mesh=mesh, in_specs=in_specs, out_specs=out_specs, check_vma=False)
```

```python
import math

import jax
import jax.numpy as jnp
from jax import lax
from jax.experimental import pallas as pl
from jax.experimental.pallas import tpu as pltpu
from jax.sharding import PartitionSpec as P

F32 = jnp.float32
BF16 = jnp.bfloat16
XS, ZS, KS, YS = 4, 8, 2, 4
MESH = pl.DeviceIdType.MESH
ROWS = 2048
COLS = 1024
CH = 256
GROUP = XS * KS
TOTAL = float(ROWS * XS * ZS * KS)
INV_TOTAL = 1.0 / TOTAL
INV_ROOT = 1.0 / math.sqrt(TOTAL)


def split(value):
    high = value.astype(BF16)
    low = (value - high.astype(F32)).astype(BF16)
    return high, low


def bdot(left, right):
    return jnp.dot(left, right, preferred_element_type=F32)


def dot3(left, right):
    (lh, ll), (rh, rl) = left, right
    return bdot(lh, rh) + (bdot(ll, rh) + bdot(lh, rl))


def fdot(left, right):
    return jnp.dot(left, right, precision=lax.Precision.HIGHEST, preferred_element_type=F32)


def ds(start, size):
    return pl.ds(pl.multiple_of(start, 8), size)


def twice(value):
    return jnp.concatenate([value, value], axis=1)


def eliminate(work, first):
    row = lax.broadcasted_iota(jnp.int32, (8, 256), 0)
    count = 4
    slabs = [work[8 * (first + q):8 * (first + q) + 8, :] for q in range(count)]
    for q in range(count):
        off = 8 * (first + q)

        def spread(slab, j):
            return jnp.broadcast_to(slab[:, off + j:off + j + 1], (8, 128))

        columns = [spread(slabs[q], j) for j in range(8)]
        diag = [[jnp.broadcast_to(columns[j][i:i + 1, :], (8, 128)) for j in range(i + 1)] for i in range(8)]
        lines = [jnp.broadcast_to(slabs[q][i:i + 1, :], (8, 256)) for i in range(8)]
        below = {p: [spread(slabs[p], j) for j in range(8)] for p in range(q + 1, count)}
        out = None
        for j in range(8):
            scale = lax.rsqrt(diag[j][j])
            lines[j] = lines[j] * twice(scale)
            low = [None] * (j + 1) + [diag[i][j] * scale for i in range(j + 1, 8)]
            for i in range(j + 1, 8):
                for m in range(j + 1, i + 1):
                    diag[i][m] = diag[i][m] - low[i] * low[m]
                lines[i] = lines[i] - twice(low[i]) * lines[j]
            for p in range(q + 1, count):
                factor = below[p][j] * scale
                for m in range(j + 1, 8):
                    below[p][m] = below[p][m] - factor * low[m]
                slabs[p] = slabs[p] - twice(factor) * lines[j]
            out = lines[j] if out is None else jnp.where(row == j, lines[j], out)
        slabs[q] = out
        work[off:off + 8, :] = out
    end = 8 * (first + count)
    if end < 128:
        done = work[8 * first:end, :]
        work[end:, :] = work[end:, :] - fdot(done[:, :128].T[end:, :], done)


def comm_kernel(
    a_hbm, t_hbm, basis_out, coeff_out,
    abuf, tbuf, ahi, alo, th, tl, ypart, rs, yfull,
    c2, cf, ccore, cx, cz, g2, gf, gg, gz, gy, gt, work, inv, bbuf, obuf,
    load_sem, rs_send, rs_recv, ag_send, ag_recv,
    core_send, core_recv, x_send, x_recv, z_send, z_recv,
    gg_send, gg_recv, gz_send, gz_recv, gy_send, gy_recv, out_sem,
):
    r = lax.axis_index("row")
    c = lax.axis_index("col")
    x, z, k = r // (ZS * KS), (r // KS) % ZS, r % KS
    g = x * KS + k

    def row_of(xx, zz, kk):
        return xx * (ZS * KS) + zz * KS + kk

    def chunk(step):
        return lax.rem(c + step, YS)

    def base(d, j):
        return d * (YS * CH) + j * CH

    def remote(src, dst, ssem, rsem, **where):
        return pltpu.make_async_remote_copy(
            src_ref=src, dst_ref=dst, send_sem=ssem, recv_sem=rsem,
            device_id=where, device_id_type=MESH)

    sends = []

    def go(copy):
        copy.start()
        sends.append(copy)

    def start(make, count):
        for o in range(1, count):
            go(make(o))

    def arrive(make, count):
        for o in range(1, count):
            make(o).wait_recv()

    barrier = pltpu.get_barrier_semaphore()
    for o in range(1, ZS):
        pl.semaphore_signal(barrier, inc=1, device_id={"row": row_of(x, lax.rem(z + o, ZS), k)}, device_id_type=MESH)
    for o in range(1, GROUP):
        gp = lax.rem(g + o, GROUP)
        pl.semaphore_signal(barrier, inc=1, device_id={"row": row_of(gp // KS, z, gp % KS)}, device_id_type=MESH)
    for o in range(1, YS):
        pl.semaphore_signal(barrier, inc=1, device_id={"col": chunk(o)}, device_id_type=MESH)

    units = [(0, 2), (1, 2), (1, 1), (0, 3), (0, 1), (1, 3), (0, 0), (1, 0)]
    t_loads = [pltpu.make_async_copy(t_hbm.at[p], tbuf.at[p], load_sem.at[8 + p]) for p in range(2)]
    loads = {}
    for i, (h, step) in enumerate(units):
        rows = ds(base(h, chunk(step)), CH)
        loads[h, step] = pltpu.make_async_copy(a_hbm.at[rows], abuf.at[rows], load_sem.at[i])
    t_loads[0].start()
    t_loads[1].start()
    for unit in units:
        loads[unit].start()
    for p in range(2):
        t_loads[p].wait()
        high, low = split(tbuf[p])
        th[:, p * 128:(p + 1) * 128] = high
        tl[:, p * 128:(p + 1) * 128] = low

    steps = (1, 3)

    def to(d):
        return chunk(steps[d])

    def relay(p, d):
        return remote(ypart.at[p, ds(base(d, chunk(2)), CH)], rs.at[p, d, 0],
                      rs_send.at[p, d, 0], rs_recv.at[p, d, 0], col=to(d))

    def direct(p, d):
        return remote(ypart.at[p, ds(base(1 - d, to(d)), CH)], rs.at[p, d, 1],
                      rs_send.at[p, d, 1], rs_recv.at[p, d, 1], col=to(d))

    def relayed(p, d):
        return remote(rs.at[p, d, 0], rs.at[p, d, 2], rs_send.at[p, d, 2], rs_recv.at[p, d, 2], col=to(d))

    def pass_on(p):
        for d in range(2):
            relay(p, d).wait_recv()
            rs[p, d, 0] = rs[p, d, 0] + ypart[p, ds(base(d, to(d)), CH), :]
            go(relayed(p, d))

    def own_sum(p):
        for h in range(2):
            direct(p, 1 - h).wait_recv()
            relayed(p, h).wait_recv()
            rows = ds(base(h, c), CH)
            yfull[p, rows, :] = (rs[p, h, 2] + rs[p, 1 - h, 1]) + ypart[p, rows, :]

    def gather(p, d, h):
        ref = yfull.at[p, ds(base(h, c), CH)]
        return remote(ref, ref, ag_send.at[p, d, h], ag_recv.at[p, d, h], col=to(d))

    def gather_on(p, d):
        ref = yfull.at[p, ds(base(d, to(1 - d)), CH)]
        return remote(ref, ref, ag_send.at[p, d, 2], ag_recv.at[p, d, 2], col=to(d))

    def sketch(h, step):
        loads[h, step].wait()
        rows = ds(base(h, chunk(step)), CH)
        high, low = split(abuf[rows, :])
        ahi[rows, :] = high
        alo[rows, :] = low
        part = dot3((high, low), (th[...], tl[...]))
        ypart[0, rows, :] = part[:, :128]
        ypart[1, rows, :] = part[:, 128:]

    def g_rows(p, index):
        return ds(index * (16 * (p + 1)), 16 * (p + 1))

    def g_peer(o):
        gp = lax.rem(g + o, GROUP)
        return gp, row_of(gp // KS, z, gp % KS)

    def g_copy(p):
        def make(o):
            gp, row = g_peer(o)
            return remote(g2.at[p, g_rows(p, gp)], gg.at[p, o - 1, g_rows(p, 0)],
                          gg_send.at[p, 0, o - 1], gg_recv.at[p, 0, o - 1], row=row)
        return make

    def gz_copy(p):
        def make(o):
            return remote(gz.at[p, z, g_rows(p, 0)], gz.at[p, z, g_rows(p, 0)], gz_send.at[p, o - 1], gz_recv.at[p, o - 1],
                          row=row_of(x, lax.rem(z + o, ZS), k))
        return make

    def gz_from(p):
        def make(o):
            slot = gz.at[p, lax.rem(z + (ZS - o), ZS), g_rows(p, 0)]
            return remote(slot, slot, gz_send.at[p, o - 1], gz_recv.at[p, o - 1], row=row_of(x, lax.rem(z + o, ZS), k))
        return make

    def gy_copy(p):
        def make(o):
            return remote(gt.at[p, g_rows(p, 0)], gy.at[p, o - 1, g_rows(p, 0)],
                          gy_send.at[p, o - 1], gy_recv.at[p, o - 1], col=chunk(o))
        return make

    def g_back(p):
        def make(o):
            ref = gf.at[p, g_rows(p, g)]
            return remote(ref, ref, gg_send.at[p, 1, o - 1], gg_recv.at[p, 1, o - 1], row=g_peer(o)[1])
        return make

    def own_rows(p):
        return jnp.concatenate([yfull[p, ds(base(h, c), CH), :] for h in range(2)], axis=0)

    def gram_local(p):
        own = own_rows(p)
        right = split(own) if p == 0 else split(jnp.concatenate([own_rows(0), own], axis=1))
        gram = dot3(split(own.T), right)
        for q in range(p + 1):
            g2[p, q * 128:(q + 1) * 128, :] = gram[:, q * 128:(q + 1) * 128]
        start(g_copy(p), GROUP)

    def g_stage1(p):
        arrive(g_copy(p), GROUP)
        total = g2[p, g_rows(p, g), :]
        for o in range(GROUP - 1):
            total = total + gg[p, o, g_rows(p, 0), :]
        gz[p, z, g_rows(p, 0), :] = total
        start(gz_copy(p), ZS)

    def g_stage2(p):
        arrive(gz_from(p), ZS)
        total = gz[p, 0, g_rows(p, 0), :]
        for o in range(1, ZS):
            total = total + gz[p, o, g_rows(p, 0), :]
        gt[p, g_rows(p, 0), :] = total
        start(gy_copy(p), YS)

    def g_stage3(p):
        arrive(gy_copy(p), YS)
        rows = g_rows(p, 0)
        gf[p, g_rows(p, g), :] = (gt[p, rows, :] + gy[p, 1, rows, :]) + (gy[p, 0, rows, :] + gy[p, 2, rows, :])
        start(g_back(p), GROUP)

    def g_stage4(p):
        arrive(g_back(p), GROUP)

    def product(p, h, step, first=False):
        rows = ds(base(h, chunk(step)), CH)
        left = split(yfull[p, rows, :].T)
        for t in range(4):
            lanes = slice(t * 256, (t + 1) * 256)
            part = dot3(left, (ahi[rows, lanes], alo[rows, lanes]))
            for q in range(2):
                out = slice((2 * t + q) * 128, (2 * t + q + 1) * 128)
                if first:
                    c2[p, out, :] = part[:, q * 128:(q + 1) * 128]
                else:
                    c2[p, out, :] += part[:, q * 128:(q + 1) * 128]

    half = k * 512
    mine = ds(half, 512)
    quarter = half + x * 128
    piece = ds(quarter + z * 16, 16)
    core_peer = row_of(x, z, 1 - k)

    def core_copy(p):
        return remote(c2.at[p, ds((1 - k) * 512, 512)], ccore.at[p], core_send.at[p, 0], core_recv.at[p, 0],
                      row=core_peer)

    def core_back(p):
        return remote(cf.at[p, mine], cf.at[p, mine], core_send.at[p, 1], core_recv.at[p, 1], row=core_peer)

    def x_copy(p):
        def make(o):
            xp = lax.rem(x + o, XS)
            return remote(c2.at[p, ds(half + xp * 128, 128)], cx.at[p, o - 1],
                          x_send.at[p, 0, o - 1], x_recv.at[p, 0, o - 1], row=row_of(xp, z, k))
        return make

    def z_copy(p):
        def make(o):
            zp = lax.rem(z + o, ZS)
            return remote(c2.at[p, ds(quarter + zp * 16, 16)], cz.at[p, o - 1],
                          z_send.at[p, 0, o - 1], z_recv.at[p, 0, o - 1], row=row_of(x, zp, k))
        return make

    def z_back(p):
        def make(o):
            return remote(cf.at[p, piece], cf.at[p, piece], z_send.at[p, 1, o - 1], z_recv.at[p, 1, o - 1],
                          row=row_of(x, lax.rem(z + o, ZS), k))
        return make

    def x_back(p):
        def make(o):
            ref = cf.at[p, ds(quarter, 128)]
            return remote(ref, ref, x_send.at[p, 1, o - 1], x_recv.at[p, 1, o - 1],
                          row=row_of(lax.rem(x + o, XS), z, k))
        return make

    def c_stage1(p):
        core_copy(p).wait_recv()
        c2[p, mine, :] += ccore[p]
        start(x_copy(p), XS)

    def c_stage2(p):
        arrive(x_copy(p), XS)
        rows = ds(quarter, 128)
        c2[p, rows, :] = (c2[p, rows, :] + cx[p, 0]) + (cx[p, 1] + cx[p, 2])
        start(z_copy(p), ZS)

    def c_stage3(p):
        arrive(z_copy(p), ZS)
        total = c2[p, piece, :]
        for o in range(ZS - 1):
            total = total + cz[p, o]
        cf[p, piece, :] = total
        start(z_back(p), ZS)

    def c_stage4(p):
        arrive(z_back(p), ZS)
        start(x_back(p), XS)

    def c_stage5(p):
        arrive(x_back(p), XS)
        go(core_back(p))

    def c_stage6(p):
        core_back(p).wait_recv()

    def eye():
        shape = (128, 128)
        same = lax.broadcasted_iota(jnp.int32, shape, 0) == lax.broadcasted_iota(jnp.int32, shape, 1)
        return same.astype(F32)

    def factor_start0():
        work[0, :, :128] = gf[0, 0:128, :] * INV_TOTAL
        work[0, :, 128:] = eye()

    def factor_start1():
        cross = fdot(work[0, :, 128:], gf[1, 0:128, :].T * INV_TOTAL)
        work[1, :, :128] = gf[1, 128:256, :] * INV_TOTAL - fdot(cross.T, cross)
        work[1, :, 128:] = eye()
        inv[:128, 128:] = cross

    def factor_end():
        inv0, inv1 = work[0, :, 128:], work[1, :, 128:]
        corner = -fdot(fdot(inv1, inv[:128, 128:].T), inv0)
        inv[:128, :128] = inv0
        inv[:128, 128:] = jnp.zeros_like(inv0)
        inv[128:, :128] = corner
        inv[128:, 128:] = inv1

    def gathered(p):
        return jnp.concatenate([cf[p, t * 128:(t + 1) * 128, :] for t in range(8)], axis=1)

    basis_copies = []

    def bases():
        across = split(inv[...].T)
        for i in range(8):
            rows = slice(i * CH, (i + 1) * CH)
            y = jnp.concatenate([yfull[0, rows, :], yfull[1, rows, :]], axis=1)
            bbuf[rows, :] = dot3(split(y), across)
            copy = pltpu.make_async_copy(bbuf.at[rows], basis_out.at[rows], out_sem.at[i])
            copy.start()
            basis_copies.append(copy)

    def gathered_first(p):
        for d in range(2):
            gather(p, d, d).wait_recv()
            go(gather_on(p, d))

    def gathered_second(p):
        for d in range(2):
            gather(p, d, 1 - d).wait_recv()

    def gathered_last(p):
        for d in range(2):
            gather_on(p, d).wait_recv()

    for unit in units[:4]:
        sketch(*unit)
    pl.semaphore_wait(barrier, (YS - 1) + (GROUP - 1) + (ZS - 1))
    for make, p in ((relay, 0), (relay, 1), (direct, 0)):
        for d in range(2):
            go(make(p, d))
    for unit in units[4:]:
        sketch(*unit)
    pass_on(0)
    pass_on(1)
    for d in range(2):
        go(direct(1, d))
    own_sum(0)
    for d in range(2):
        go(gather(0, d, d))
    for d in range(2):
        go(gather(0, d, 1 - d))
    gram_local(0)
    product(0, 0, 0, True)
    product(0, 1, 0)
    g_stage1(0)
    own_sum(1)
    for d in range(2):
        go(gather(1, d, d))
    gram_local(1)
    product(1, 0, 0, True)
    product(1, 1, 0)
    gathered_first(0)
    for d in range(2):
        go(gather(1, d, 1 - d))
    product(0, 0, 3)
    product(0, 1, 1)
    g_stage1(1)
    g_stage2(0)
    gathered_second(0)
    product(0, 1, 3)
    product(0, 0, 1)
    gathered_last(0)
    product(0, 0, 2)
    product(0, 1, 2)
    go(core_copy(0))
    gathered_first(1)
    c_stage1(0)
    g_stage3(0)
    product(1, 0, 3)
    product(1, 1, 1)
    g_stage2(1)
    gathered_second(1)
    product(1, 1, 3)
    product(1, 0, 1)
    c_stage2(0)
    gathered_last(1)
    product(1, 0, 2)
    product(1, 1, 2)
    go(core_copy(1))
    g_stage4(0)
    factor_start0()
    c_stage1(1)
    g_stage3(1)
    eliminate(work.at[0], 0)
    eliminate(work.at[0], 4)
    c_stage3(0)
    eliminate(work.at[0], 8)
    c_stage2(1)
    eliminate(work.at[0], 12)
    g_stage4(1)
    factor_start1()
    c_stage4(0)
    eliminate(work.at[1], 0)
    c_stage3(1)
    eliminate(work.at[1], 4)
    eliminate(work.at[1], 8)
    eliminate(work.at[1], 12)
    c_stage5(0)
    factor_end()
    c_stage4(1)
    c_stage6(0)
    first = dot3(split(inv[:, :128]), split(gathered(0)))
    obuf[:128, :] = first[:128, :] * INV_ROOT
    obuf[128:, :] = first[128:, :]
    coeff_copy0 = pltpu.make_async_copy(obuf.at[0:128], coeff_out.at[0:128], out_sem.at[8])
    coeff_copy0.start()
    bases()
    c_stage5(1)
    c_stage6(1)
    last = dot3(split(inv[128:, 128:]), split(gathered(1)))
    obuf[128:, :] = (obuf[128:, :] + last) * INV_ROOT
    coeff_copy1 = pltpu.make_async_copy(obuf.at[128:256], coeff_out.at[128:256], out_sem.at[9])
    coeff_copy1.start()
    for copy in sends:
        copy.wait_send()
    for copy in basis_copies:
        copy.wait()
    coeff_copy0.wait()
    coeff_copy1.wait()


def per_device(snapshots, tests):
    vmem, dma = pltpu.VMEM, pltpu.SemaphoreType.DMA
    any_spec = pl.BlockSpec(memory_space=pl.ANY)
    return pl.pallas_call(
        comm_kernel,
        out_shape=(jax.ShapeDtypeStruct((ROWS, 256), F32), jax.ShapeDtypeStruct((256, COLS), F32)),
        in_specs=[any_spec, any_spec],
        out_specs=(any_spec, any_spec),
        scratch_shapes=[
            vmem((ROWS, COLS), F32), vmem((2, COLS, 128), F32), vmem((ROWS, COLS), BF16), vmem((ROWS, COLS), BF16),
            vmem((COLS, 256), BF16), vmem((COLS, 256), BF16), vmem((2, ROWS, 128), F32),
            vmem((2, 2, 3, CH, 128), F32), vmem((2, ROWS, 128), F32),
            vmem((2, 1024, 128), F32), vmem((2, 1024, 128), F32), vmem((2, 512, 128), F32),
            vmem((2, 3, 128, 128), F32), vmem((2, 7, 16, 128), F32),
            vmem((2, 256, 128), F32), vmem((2, 256, 128), F32), vmem((2, 7, 32, 128), F32),
            vmem((2, ZS, 32, 128), F32), vmem((2, 3, 32, 128), F32), vmem((2, 32, 128), F32),
            vmem((2, 128, 256), F32), vmem((256, 256), F32),
            vmem((ROWS, 256), F32), vmem((256, COLS), F32),
            dma((10,)), dma((2, 2, 3)), dma((2, 2, 3)), dma((2, 2, 3)), dma((2, 2, 3)),
            dma((2, 2)), dma((2, 2)), dma((2, 2, 3)), dma((2, 2, 3)), dma((2, 2, 7)), dma((2, 2, 7)),
            dma((2, 2, 7)), dma((2, 2, 7)), dma((2, 7)), dma((2, 7)), dma((2, 3)), dma((2, 3)), dma((10,))],
        compiler_params=pltpu.CompilerParams(collective_id=0, has_side_effects=True, vmem_limit_bytes=56 << 20),
    )(snapshots, tests)


def solution(mesh):
    in_specs = (P("row", "col"), P(None, "col", None))
    out_specs = (P("row", None), P(None, "col"))
    return jax.shard_map(per_device, mesh=mesh, in_specs=in_specs, out_specs=out_specs, check_vma=False)
```

```python
import functools
import math

import jax
import jax.numpy as jnp
from jax import lax
from jax.experimental import pallas as pl
from jax.experimental.pallas import tpu as pltpu
from jax.sharding import PartitionSpec as P

F32 = jnp.float32
BF16 = jnp.bfloat16
XS, ZS, KS, YS = 4, 8, 2, 4
MESH = pl.DeviceIdType.MESH
ROWS = 2048
COLS = 1024
CH = 256
TOTAL = float(ROWS * XS * ZS * KS)
INV_TOTAL = 1.0 / TOTAL
INV_ROOT = 1.0 / math.sqrt(TOTAL)


def split(value):
    high = value.astype(BF16)
    low = (value - high.astype(F32)).astype(BF16)
    return high, low


def bdot(left, right):
    return jnp.dot(left, right, preferred_element_type=F32)


def dot3(left, right):
    (lh, ll), (rh, rl) = left, right
    return bdot(lh, rh) + (bdot(ll, rh) + bdot(lh, rl))


def fdot(left, right):
    return jnp.dot(left, right, precision=lax.Precision.HIGHEST, preferred_element_type=F32)


def ds(start, size):
    return pl.ds(pl.multiple_of(start, 8), size)


def twice(value):
    return jnp.concatenate([value, value], axis=1)


def eliminate(work, first):
    row = lax.broadcasted_iota(jnp.int32, (8, 256), 0)
    count = 4
    slabs = [work[8 * (first + q):8 * (first + q) + 8, :] for q in range(count)]
    for q in range(count):
        off = 8 * (first + q)

        def spread(slab, j):
            return jnp.broadcast_to(slab[:, off + j:off + j + 1], (8, 128))

        columns = [spread(slabs[q], j) for j in range(8)]
        diag = [[jnp.broadcast_to(columns[j][i:i + 1, :], (8, 128)) for j in range(i + 1)] for i in range(8)]
        lines = [jnp.broadcast_to(slabs[q][i:i + 1, :], (8, 256)) for i in range(8)]
        below = {p: [spread(slabs[p], j) for j in range(8)] for p in range(q + 1, count)}
        out = None
        for j in range(8):
            scale = lax.rsqrt(diag[j][j])
            lines[j] = lines[j] * twice(scale)
            low = [None] * (j + 1) + [diag[i][j] * scale for i in range(j + 1, 8)]
            for i in range(j + 1, 8):
                for m in range(j + 1, i + 1):
                    diag[i][m] = diag[i][m] - low[i] * low[m]
                lines[i] = lines[i] - twice(low[i]) * lines[j]
            for p in range(q + 1, count):
                factor = below[p][j] * scale
                for m in range(j + 1, 8):
                    below[p][m] = below[p][m] - factor * low[m]
                slabs[p] = slabs[p] - twice(factor) * lines[j]
            out = lines[j] if out is None else jnp.where(row == j, lines[j], out)
        slabs[q] = out
        work[off:off + 8, :] = out
    end = 8 * (first + count)
    if end < 128:
        done = work[8 * first:end, :]
        work[end:, :] = work[end:, :] - fdot(done[:, :128].T[end:, :], done)


def comm_kernel(
    a_hbm, t_hbm, bbuf, obuf,
    abuf, tbuf, ahi, alo, th, tl, ypart, rs, yfull,
    c2, cf, ccore, cx, cz, g2, gf, gk, gx, gz, gy, gt, work, inv,
    load_sem, rs_send, rs_recv, ag_send, ag_recv,
    core_send, core_recv, x_send, x_recv, z_send, z_recv,
    inv_sem, gk_send, gk_recv, gx_send, gx_recv, gz_send, gz_recv, gy_send, gy_recv,
):
    r = lax.axis_index("row")
    c = lax.axis_index("col")
    x, z, k = r // (ZS * KS), (r // KS) % ZS, r % KS

    def row_of(xx, zz, kk):
        return xx * (ZS * KS) + zz * KS + kk

    def chunk(step):
        return lax.rem(c + step, YS)

    def base(d, j):
        return d * (YS * CH) + j * CH

    def remote(src, dst, ssem, rsem, **where):
        return pltpu.make_async_remote_copy(
            src_ref=src, dst_ref=dst, send_sem=ssem, recv_sem=rsem,
            device_id=where, device_id_type=MESH)

    sends = []
    role_sends = ([], [])

    def go(copy):
        copy.start()
        sends.append(copy)

    def go_role(make, core):
        make().start()
        role_sends[core].append(make)

    def start(make, count, core):
        for o in sorted(range(1, count), key=lambda o: -min(o, count - o)):
            go_role(functools.partial(make, o), core)

    def arrive(make, count):
        for o in range(1, count):
            make(o).wait_recv()

    def role(core):
        return pl.when(k == core)

    barrier = pltpu.get_barrier_semaphore()
    for o in (4, 3, 5, 2, 6, 1, 7):
        pl.semaphore_signal(barrier, inc=1, device_id={"row": row_of(x, lax.rem(z + o, ZS), k)}, device_id_type=MESH)
    for o in range(1, XS):
        pl.semaphore_signal(barrier, inc=1, device_id={"row": row_of(lax.rem(x + o, XS), z, k)}, device_id_type=MESH)
    pl.semaphore_signal(barrier, inc=1, device_id={"row": row_of(x, z, 1 - k)}, device_id_type=MESH)
    for o in range(1, YS):
        pl.semaphore_signal(barrier, inc=1, device_id={"col": chunk(o)}, device_id_type=MESH)

    units = [(0, 2), (1, 2), (1, 1), (0, 3), (0, 1), (1, 3), (0, 0), (1, 0)]
    t_loads = [pltpu.make_async_copy(t_hbm.at[p], tbuf.at[p], load_sem.at[8 + p]) for p in range(2)]
    loads = {}
    for i, (h, step) in enumerate(units):
        rows = ds(base(h, chunk(step)), CH)
        loads[h, step] = pltpu.make_async_copy(a_hbm.at[rows], abuf.at[rows], load_sem.at[i])
    t_loads[0].start()
    t_loads[1].start()
    for unit in units:
        loads[unit].start()
    for p in range(2):
        t_loads[p].wait()
        high, low = split(tbuf[p])
        th[:, p * 128:(p + 1) * 128] = high
        tl[:, p * 128:(p + 1) * 128] = low

    steps = (1, 3)

    def to(d):
        return chunk(steps[d])

    def relay(p, d):
        return remote(ypart.at[p, ds(base(d, chunk(2)), CH)], rs.at[p, d, 0],
                      rs_send.at[p, d, 0], rs_recv.at[p, d, 0], col=to(d))

    def direct(p, d):
        return remote(ypart.at[p, ds(base(1 - d, to(d)), CH)], rs.at[p, d, 1],
                      rs_send.at[p, d, 1], rs_recv.at[p, d, 1], col=to(d))

    def relayed(p, d):
        return remote(rs.at[p, d, 0], rs.at[p, d, 2], rs_send.at[p, d, 2], rs_recv.at[p, d, 2], col=to(d))

    def pass_on(p):
        for d in range(2):
            relay(p, d).wait_recv()
            rs[p, d, 0] = rs[p, d, 0] + ypart[p, ds(base(d, to(d)), CH), :]
            go(relayed(p, d))

    def own_sum(p):
        for h in range(2):
            direct(p, 1 - h).wait_recv()
            relayed(p, h).wait_recv()
            rows = ds(base(h, c), CH)
            yfull[p, rows, :] = (rs[p, h, 2] + rs[p, 1 - h, 1]) + ypart[p, rows, :]

    def gather(p, d, h):
        ref = yfull.at[p, ds(base(h, c), CH)]
        return remote(ref, ref, ag_send.at[p, d, h], ag_recv.at[p, d, h], col=to(d))

    def gather_on(p, d):
        ref = yfull.at[p, ds(base(d, to(1 - d)), CH)]
        return remote(ref, ref, ag_send.at[p, d, 2], ag_recv.at[p, d, 2], col=to(d))

    def sketch(h, step):
        loads[h, step].wait()
        rows = ds(base(h, chunk(step)), CH)
        high, low = split(abuf[rows, :])
        ahi[rows, :] = high
        alo[rows, :] = low
        part = dot3((high, low), (th[...], tl[...]))
        ypart[0, rows, :] = part[:, :128]
        ypart[1, rows, :] = part[:, 128:]

    def g_rows(p, index, size=32):
        return ds(index * (size * (p + 1)), size * (p + 1))

    core_peer = row_of(x, z, 1 - k)

    def gk_copy(p):
        return remote(g2.at[p, g_rows(p, 0, 128)], gk.at[p, g_rows(p, 0, 128)], gk_send.at[p], gk_recv.at[p], row=core_peer)

    def gx_copy(p):
        def make(o):
            xp = lax.rem(x + o, XS)
            return remote(g2.at[p, g_rows(p, xp)], gx.at[p, o - 1, g_rows(p, 0)],
                          gx_send.at[p, 0, o - 1], gx_recv.at[p, 0, o - 1], row=row_of(xp, z, k))
        return make

    def gx_back(p):
        def make(o):
            ref = gf.at[p, g_rows(p, x)]
            return remote(ref, ref, gx_send.at[p, 1, o - 1], gx_recv.at[p, 1, o - 1],
                          row=row_of(lax.rem(x + o, XS), z, k))
        return make

    def gz_copy(p):
        def make(o):
            slot = gz.at[p, z, g_rows(p, 0)]
            return remote(slot, slot, gz_send.at[p, o - 1], gz_recv.at[p, o - 1], row=row_of(x, lax.rem(z + o, ZS), k))
        return make

    def gz_from(p):
        def make(o):
            slot = gz.at[p, lax.rem(z + (ZS - o), ZS), g_rows(p, 0)]
            return remote(slot, slot, gz_send.at[p, o - 1], gz_recv.at[p, o - 1], row=row_of(x, lax.rem(z + o, ZS), k))
        return make

    def gy_copy(p):
        def make(o):
            return remote(gt.at[p, g_rows(p, 0)], gy.at[p, o - 1, g_rows(p, 0)],
                          gy_send.at[p, o - 1], gy_recv.at[p, o - 1], col=chunk(o))
        return make

    def own_rows(p):
        return jnp.concatenate([yfull[p, ds(base(h, c), CH), :] for h in range(2)], axis=0)

    def gram_local(p):
        own = own_rows(p)
        right = split(own) if p == 0 else split(jnp.concatenate([own_rows(0), own], axis=1))
        gram = dot3(split(own.T), right)
        for q in range(p + 1):
            g2[p, q * 128:(q + 1) * 128, :] = gram[:, q * 128:(q + 1) * 128]

        @role(0)
        def _():
            go_role(functools.partial(gk_copy, p), 0)

    def g_core(p):
        @role(1)
        def _():
            gk_copy(p).wait_recv()
            rows = g_rows(p, 0, 128)
            g2[p, rows, :] = g2[p, rows, :] + gk[p, rows, :]
            start(gx_copy(p), XS, 1)

    def g_x(p):
        @role(1)
        def _():
            arrive(gx_copy(p), XS)
            rows = g_rows(p, 0)
            total = (g2[p, g_rows(p, x), :] + gx[p, 1, rows, :]) + (gx[p, 0, rows, :] + gx[p, 2, rows, :])
            gz[p, z, rows, :] = total
            start(gz_copy(p), ZS, 1)

    def g_z(p):
        @role(1)
        def _():
            arrive(gz_from(p), ZS)
            total = gz[p, 0, g_rows(p, 0), :]
            for o in range(1, ZS):
                total = total + gz[p, o, g_rows(p, 0), :]
            gt[p, g_rows(p, 0), :] = total
            start(gy_copy(p), YS, 1)

    def g_y(p):
        @role(1)
        def _():
            arrive(gy_copy(p), YS)
            rows = g_rows(p, 0)
            gf[p, g_rows(p, x), :] = (gt[p, rows, :] + gy[p, 1, rows, :]) + (gy[p, 0, rows, :] + gy[p, 2, rows, :])
            start(gx_back(p), XS, 1)

    def g_x_back(p):
        @role(1)
        def _():
            arrive(gx_back(p), XS)

    def product(p, h, step, first=False):
        rows = ds(base(h, chunk(step)), CH)
        left = split(yfull[p, rows, :].T)
        for t in range(4):
            lanes = slice(t * 256, (t + 1) * 256)
            part = dot3(left, (ahi[rows, lanes], alo[rows, lanes]))
            for q in range(2):
                out = slice((2 * t + q) * 128, (2 * t + q + 1) * 128)
                if first:
                    c2[p, out, :] = part[:, q * 128:(q + 1) * 128]
                else:
                    c2[p, out, :] += part[:, q * 128:(q + 1) * 128]

    quarter = x * 256
    piece = ds(quarter + z * 32, 32)

    def core_copy(p):
        return remote(c2.at[p], ccore.at[p], core_send.at[p, 0], core_recv.at[p, 0], row=core_peer)

    def core_back(p):
        return remote(cf.at[p], cf.at[p], core_send.at[p, 1], core_recv.at[p, 1], row=core_peer)

    def x_copy(p):
        def make(o):
            xp = lax.rem(x + o, XS)
            return remote(c2.at[p, ds(xp * 256, 256)], cx.at[p, o - 1],
                          x_send.at[p, 0, o - 1], x_recv.at[p, 0, o - 1], row=row_of(xp, z, k))
        return make

    def z_copy(p):
        def make(o):
            zp = lax.rem(z + o, ZS)
            return remote(c2.at[p, ds(quarter + zp * 32, 32)], cz.at[p, o - 1],
                          z_send.at[p, 0, o - 1], z_recv.at[p, 0, o - 1], row=row_of(x, zp, k))
        return make

    def z_back(p):
        def make(o):
            return remote(cf.at[p, piece], cf.at[p, piece], z_send.at[p, 1, o - 1], z_recv.at[p, 1, o - 1],
                          row=row_of(x, lax.rem(z + o, ZS), k))
        return make

    def x_back(p):
        def make(o):
            ref = cf.at[p, ds(quarter, 256)]
            return remote(ref, ref, x_send.at[p, 1, o - 1], x_recv.at[p, 1, o - 1],
                          row=row_of(lax.rem(x + o, XS), z, k))
        return make

    def c_send(p):
        @role(1)
        def _():
            go_role(functools.partial(core_copy, p), 1)

    def c_core(p):
        @role(0)
        def _():
            core_copy(p).wait_recv()
            c2[p] = c2[p] + ccore[p]
            start(x_copy(p), XS, 0)

    def c_x(p):
        @role(0)
        def _():
            arrive(x_copy(p), XS)
            rows = ds(quarter, 256)
            c2[p, rows, :] = (c2[p, rows, :] + cx[p, 0]) + (cx[p, 1] + cx[p, 2])
            start(z_copy(p), ZS, 0)

    def c_z(p):
        @role(0)
        def _():
            arrive(z_copy(p), ZS)
            total = c2[p, piece, :]
            for o in range(ZS - 1):
                total = total + cz[p, o]
            cf[p, piece, :] = total
            start(z_back(p), ZS, 0)

    def c_z_back(p):
        @role(0)
        def _():
            arrive(z_back(p), ZS)
            start(x_back(p), XS, 0)

    def c_x_back(p):
        @role(0)
        def _():
            arrive(x_back(p), XS)
            go_role(functools.partial(core_back, p), 0)

    def c_core_back(p):
        @role(1)
        def _():
            core_back(p).wait_recv()

    def eye():
        shape = (128, 128)
        same = lax.broadcasted_iota(jnp.int32, shape, 0) == lax.broadcasted_iota(jnp.int32, shape, 1)
        return same.astype(F32)

    def factor_start0():
        work[0, :, :128] = gf[0, 0:128, :] * INV_TOTAL
        work[0, :, 128:] = eye()

    def factor_start1():
        cross = fdot(work[0, :, 128:], gf[1, 0:128, :].T * INV_TOTAL)
        work[1, :, :128] = gf[1, 128:256, :] * INV_TOTAL - fdot(cross.T, cross)
        work[1, :, 128:] = eye()
        inv[:128, 128:] = cross

    def factor_end():
        inv0, inv1 = work[0, :, 128:], work[1, :, 128:]
        corner = -fdot(fdot(inv1, inv[:128, 128:].T), inv0)
        inv[:128, :128] = inv0
        inv[:128, 128:] = jnp.zeros_like(inv0)
        inv[128:, :128] = corner
        inv[128:, 128:] = inv1

    def inverse_copy():
        return remote(inv, inv, inv_sem.at[0], inv_sem.at[1], row=core_peer)

    def gathered(p):
        return jnp.concatenate([cf[p, t * 128:(t + 1) * 128, :] for t in range(8)], axis=1)

    def bases():
        across = split(inv[...].T)
        for i in range(8):
            rows = slice(i * CH, (i + 1) * CH)
            y = jnp.concatenate([yfull[0, rows, :], yfull[1, rows, :]], axis=1)
            bbuf[rows, :] = dot3(split(y), across)

    def gathered_first(p):
        for d in range(2):
            gather(p, d, d).wait_recv()
            go(gather_on(p, d))

    def gathered_second(p):
        for d in range(2):
            gather(p, d, 1 - d).wait_recv()

    def gathered_last(p):
        for d in range(2):
            gather_on(p, d).wait_recv()

    for unit in units[:4]:
        sketch(*unit)
    pl.semaphore_wait(barrier, (YS - 1) + (XS - 1) + (KS - 1) + (ZS - 1))
    for make in (relay, direct):
        for d in range(2):
            go(make(0, d))
    for unit in units[4:6]:
        sketch(*unit)
    for d in range(2):
        go(relay(1, d))
    for unit in units[6:]:
        sketch(*unit)
    pass_on(0)
    for d in range(2):
        go(direct(1, d))
    pass_on(1)
    own_sum(0)
    for d in range(2):
        go(gather(0, d, d))
    for d in range(2):
        go(gather(0, d, 1 - d))
    gram_local(0)
    product(0, 0, 0, True)
    product(0, 1, 0)
    g_core(0)
    own_sum(1)
    for d in range(2):
        go(gather(1, d, d))
    gram_local(1)
    g_x(0)
    g_core(1)
    product(1, 0, 0, True)
    product(1, 1, 0)
    gathered_first(0)
    for d in range(2):
        go(gather(1, d, 1 - d))
    product(0, 0, 3)
    product(0, 1, 1)
    gathered_second(0)
    product(0, 1, 3)
    product(0, 0, 1)
    g_x(1)
    g_z(0)
    gathered_last(0)
    product(0, 0, 2)
    product(0, 1, 2)
    c_send(0)
    c_core(0)
    gathered_first(1)
    g_y(0)
    product(1, 0, 3)
    product(1, 1, 1)
    g_z(1)
    gathered_second(1)
    product(1, 1, 3)
    product(1, 0, 1)
    g_x_back(0)
    c_x(0)
    g_y(1)

    @role(1)
    def _():
        factor_start0()
        eliminate(work.at[0], 0)

    gathered_last(1)
    product(1, 0, 2)
    product(1, 1, 2)
    c_send(1)

    def first():
        both = dot3(split(inv[:, :128]), split(gathered(0)))
        obuf[:128, :] = both[:128, :] * INV_ROOT
        obuf[128:, :] = both[128:, :]

    c_core(1)
    c_z(0)
    c_x(1)
    c_z_back(0)
    c_z(1)
    c_x_back(0)
    c_z_back(1)

    @role(1)
    def _():
        for i in (4, 8, 12):
            eliminate(work.at[0], i)

    g_x_back(1)

    @role(1)
    def _():
        factor_start1()
        for i in (0, 4, 8, 12):
            eliminate(work.at[1], i)
        factor_end()
        go_role(inverse_copy, 1)

    @role(0)
    def _():
        inverse_copy().wait_recv()

    c_core_back(0)
    bases()
    first()
    c_x_back(1)
    c_core_back(1)
    last = dot3(split(inv[128:, 128:]), split(gathered(1)))
    obuf[128:, :] = (obuf[128:, :] + last) * INV_ROOT
    for core in range(2):
        @role(core)
        def _():
            for make in role_sends[core]:
                make().wait_send()

    for copy in sends:
        copy.wait_send()


def per_device(snapshots, tests):
    vmem, dma = pltpu.VMEM, pltpu.SemaphoreType.DMA
    any_spec = pl.BlockSpec(memory_space=pl.ANY)
    return pl.pallas_call(
        comm_kernel,
        out_shape=(vmem((ROWS, 256), F32), vmem((256, COLS), F32)),
        in_specs=[any_spec, any_spec],
        out_specs=(pl.BlockSpec(memory_space=vmem), pl.BlockSpec(memory_space=vmem)),
        scratch_shapes=[
            vmem((ROWS, COLS), F32), vmem((2, COLS, 128), F32), vmem((ROWS, COLS), BF16), vmem((ROWS, COLS), BF16),
            vmem((COLS, 256), BF16), vmem((COLS, 256), BF16), vmem((2, ROWS, 128), F32),
            vmem((2, 2, 3, CH, 128), F32), vmem((2, ROWS, 128), F32),
            vmem((2, 1024, 128), F32), vmem((2, 1024, 128), F32), vmem((2, 1024, 128), F32),
            vmem((2, 3, 256, 128), F32), vmem((2, 7, 32, 128), F32),
            vmem((2, 256, 128), F32), vmem((2, 256, 128), F32), vmem((2, 256, 128), F32), vmem((2, 3, 64, 128), F32),
            vmem((2, ZS, 64, 128), F32), vmem((2, 3, 64, 128), F32), vmem((2, 64, 128), F32),
            vmem((2, 128, 256), F32), vmem((256, 256), F32),
            dma((10,)), dma((2, 2, 3)), dma((2, 2, 3)), dma((2, 2, 3)), dma((2, 2, 3)),
            dma((2, 2)), dma((2, 2)), dma((2, 2, 3)), dma((2, 2, 3)), dma((2, 2, 7)), dma((2, 2, 7)), dma((2,)),
            dma((2,)), dma((2,)), dma((2, 2, 3)), dma((2, 2, 3)), dma((2, 7)), dma((2, 7)), dma((2, 3)), dma((2, 3))],
        compiler_params=pltpu.CompilerParams(collective_id=0, has_side_effects=True, vmem_limit_bytes=52 << 20),
    )(snapshots, tests)


def solution(mesh):
    in_specs = (P("row", "col"), P(None, "col", None))
    out_specs = (P("row", None), P(None, "col"))
    return jax.shard_map(per_device, mesh=mesh, in_specs=in_specs, out_specs=out_specs, check_vma=False)
```

```python
import functools
import math

import jax
import jax.numpy as jnp
from jax import lax
from jax.experimental import pallas as pl
from jax.experimental.pallas import tpu as pltpu
from jax.sharding import PartitionSpec as P

F32 = jnp.float32
BF16 = jnp.bfloat16
XS, ZS, KS, YS = 4, 8, 2, 4
MESH = pl.DeviceIdType.MESH
ROWS = 2048
COLS = 1024
CH = 256
TOTAL = float(ROWS * XS * ZS * KS)
INV_TOTAL = 1.0 / TOTAL
INV_ROOT = 1.0 / math.sqrt(TOTAL)


def split(value):
    high = value.astype(BF16)
    low = (value - high.astype(F32)).astype(BF16)
    return high, low


def bdot(left, right):
    return jnp.dot(left, right, preferred_element_type=F32)


def dot3(left, right):
    (lh, ll), (rh, rl) = left, right
    return bdot(lh, rh) + (bdot(ll, rh) + bdot(lh, rl))


def fdot(left, right):
    return jnp.dot(left, right, precision=lax.Precision.HIGHEST, preferred_element_type=F32)


def ds(start, size):
    return pl.ds(pl.multiple_of(start, 8), size)


def twice(value):
    return jnp.concatenate([value, value], axis=1)


def eliminate(work, first):
    row = lax.broadcasted_iota(jnp.int32, (8, 256), 0)
    count = 4
    slabs = [work[8 * (first + q):8 * (first + q) + 8, :] for q in range(count)]
    for q in range(count):
        off = 8 * (first + q)

        def spread(slab, j):
            return jnp.broadcast_to(slab[:, off + j:off + j + 1], (8, 128))

        columns = [spread(slabs[q], j) for j in range(8)]
        diag = [[jnp.broadcast_to(columns[j][i:i + 1, :], (8, 128)) for j in range(i + 1)] for i in range(8)]
        lines = [jnp.broadcast_to(slabs[q][i:i + 1, :], (8, 256)) for i in range(8)]
        below = {p: [spread(slabs[p], j) for j in range(8)] for p in range(q + 1, count)}
        out = None
        for j in range(8):
            scale = lax.rsqrt(diag[j][j])
            lines[j] = lines[j] * twice(scale)
            low = [None] * (j + 1) + [diag[i][j] * scale for i in range(j + 1, 8)]
            for i in range(j + 1, 8):
                for m in range(j + 1, i + 1):
                    diag[i][m] = diag[i][m] - low[i] * low[m]
                lines[i] = lines[i] - twice(low[i]) * lines[j]
            for p in range(q + 1, count):
                factor = below[p][j] * scale
                for m in range(j + 1, 8):
                    below[p][m] = below[p][m] - factor * low[m]
                slabs[p] = slabs[p] - twice(factor) * lines[j]
            out = lines[j] if out is None else jnp.where(row == j, lines[j], out)
        slabs[q] = out
        work[off:off + 8, :] = out
    end = 8 * (first + count)
    if end < 128:
        done = work[8 * first:end, :]
        work[end:, :] = work[end:, :] - fdot(done[:, :128].T[end:, :], done)


def comm_kernel(
    a_hbm, t_hbm, bbuf, obuf,
    abuf, tbuf, ahi, alo, th, tl, ypart, rs, yfull,
    c2, cf, ccore, cx, cz, g2, gf, gk, gx, gz, gy, gt, work, inv,
    load_sem, rs_send, rs_recv, ag_send, ag_recv,
    core_send, core_recv, x_send, x_recv, z_send, z_recv,
    inv_sem, gk_send, gk_recv, gx_send, gx_recv, gz_send, gz_recv, gy_send, gy_recv,
):
    r = lax.axis_index("row")
    c = lax.axis_index("col")
    x, z, k = r // (ZS * KS), (r // KS) % ZS, r % KS

    def row_of(xx, zz, kk):
        return xx * (ZS * KS) + zz * KS + kk

    def chunk(step):
        return lax.rem(c + step, YS)

    def base(d, j):
        return d * (YS * CH) + j * CH

    def remote(src, dst, ssem, rsem, **where):
        return pltpu.make_async_remote_copy(
            src_ref=src, dst_ref=dst, send_sem=ssem, recv_sem=rsem,
            device_id=where, device_id_type=MESH)

    sends = []
    role_sends = ([], [])

    def go(copy):
        copy.start()
        sends.append(copy)

    def go_role(make, core):
        make().start()
        role_sends[core].append(make)

    def start(make, count, core):
        for o in sorted(range(1, count), key=lambda o: -min(o, count - o)):
            go_role(functools.partial(make, o), core)

    def arrive(make, count):
        for o in range(1, count):
            make(o).wait_recv()

    def role(core):
        return pl.when(k == core)

    barrier = pltpu.get_barrier_semaphore()
    for o in (4, 3, 5, 2, 6, 1, 7):
        pl.semaphore_signal(barrier, inc=1, device_id={"row": row_of(x, lax.rem(z + o, ZS), k)}, device_id_type=MESH)
    for o in range(1, XS):
        pl.semaphore_signal(barrier, inc=1, device_id={"row": row_of(lax.rem(x + o, XS), z, k)}, device_id_type=MESH)
    pl.semaphore_signal(barrier, inc=1, device_id={"row": row_of(x, z, 1 - k)}, device_id_type=MESH)
    for o in range(1, YS):
        pl.semaphore_signal(barrier, inc=1, device_id={"col": chunk(o)}, device_id_type=MESH)

    units = [(0, 2), (1, 2), (1, 1), (0, 3), (0, 1), (1, 3), (0, 0), (1, 0)]
    t_loads = [pltpu.make_async_copy(t_hbm.at[p], tbuf.at[p], load_sem.at[8 + p]) for p in range(2)]
    loads = {}
    for i, (h, step) in enumerate(units):
        rows = ds(base(h, chunk(step)), CH)
        loads[h, step] = pltpu.make_async_copy(a_hbm.at[rows], abuf.at[rows], load_sem.at[i])
    t_loads[0].start()
    t_loads[1].start()
    for unit in units[:2]:
        loads[unit].start()
    for p in range(2):
        t_loads[p].wait()
        high, low = split(tbuf[p])
        th[:, p * 128:(p + 1) * 128] = high
        tl[:, p * 128:(p + 1) * 128] = low

    steps = (1, 3)

    def to(d):
        return chunk(steps[d])

    def relay(p, d):
        return remote(ypart.at[p, ds(base(d, chunk(2)), CH)], rs.at[p, d, 0],
                      rs_send.at[p, d, 0], rs_recv.at[p, d, 0], col=to(d))

    def direct(p, d):
        return remote(ypart.at[p, ds(base(1 - d, to(d)), CH)], rs.at[p, d, 1],
                      rs_send.at[p, d, 1], rs_recv.at[p, d, 1], col=to(d))

    def relayed(p, d):
        return remote(rs.at[p, d, 0], rs.at[p, d, 2], rs_send.at[p, d, 2], rs_recv.at[p, d, 2], col=to(d))

    def pass_on(p):
        for d in range(2):
            relay(p, d).wait_recv()
            rs[p, d, 0] = rs[p, d, 0] + ypart[p, ds(base(d, to(d)), CH), :]
            go(relayed(p, d))

    def own_sum(p):
        for h in range(2):
            direct(p, 1 - h).wait_recv()
            relayed(p, h).wait_recv()
            rows = ds(base(h, c), CH)
            yfull[p, rows, :] = (rs[p, h, 2] + rs[p, 1 - h, 1]) + ypart[p, rows, :]

    def gather(p, d, h):
        ref = yfull.at[p, ds(base(h, c), CH)]
        return remote(ref, ref, ag_send.at[p, d, h], ag_recv.at[p, d, h], col=to(d))

    def gather_on(p, d):
        ref = yfull.at[p, ds(base(d, to(1 - d)), CH)]
        return remote(ref, ref, ag_send.at[p, d, 2], ag_recv.at[p, d, 2], col=to(d))

    def sketch(h, step):
        if (h, step) != units[0]:
            loads[h, step].wait()
        rows = ds(base(h, chunk(step)), CH)
        high, low = split(abuf[rows, :])
        ahi[rows, :] = high
        alo[rows, :] = low
        part = dot3((high, low), (th[...], tl[...]))
        ypart[0, rows, :] = part[:, :128]
        ypart[1, rows, :] = part[:, 128:]

    def g_rows(p, index, size=32):
        return ds(index * (size * (p + 1)), size * (p + 1))

    core_peer = row_of(x, z, 1 - k)

    def gk_copy(p):
        return remote(g2.at[p, g_rows(p, 0, 128)], gk.at[p, g_rows(p, 0, 128)], gk_send.at[p], gk_recv.at[p], row=core_peer)

    def gx_copy(p):
        def make(o):
            xp = lax.rem(x + o, XS)
            return remote(g2.at[p, g_rows(p, xp)], gx.at[p, o - 1, g_rows(p, 0)],
                          gx_send.at[p, 0, o - 1], gx_recv.at[p, 0, o - 1], row=row_of(xp, z, k))
        return make

    def gx_back(p):
        def make(o):
            ref = gf.at[p, g_rows(p, x)]
            return remote(ref, ref, gx_send.at[p, 1, o - 1], gx_recv.at[p, 1, o - 1],
                          row=row_of(lax.rem(x + o, XS), z, k))
        return make

    def gz_copy(p):
        def make(o):
            slot = gz.at[p, z, g_rows(p, 0)]
            return remote(slot, slot, gz_send.at[p, o - 1], gz_recv.at[p, o - 1], row=row_of(x, lax.rem(z + o, ZS), k))
        return make

    def gz_from(p):
        def make(o):
            slot = gz.at[p, lax.rem(z + (ZS - o), ZS), g_rows(p, 0)]
            return remote(slot, slot, gz_send.at[p, o - 1], gz_recv.at[p, o - 1], row=row_of(x, lax.rem(z + o, ZS), k))
        return make

    def gy_copy(p):
        def make(o):
            return remote(gt.at[p, g_rows(p, 0)], gy.at[p, o - 1, g_rows(p, 0)],
                          gy_send.at[p, o - 1], gy_recv.at[p, o - 1], col=chunk(o))
        return make

    def own_rows(p):
        return jnp.concatenate([yfull[p, ds(base(h, c), CH), :] for h in range(2)], axis=0)

    def gram_local(p):
        own = own_rows(p)
        right = split(own) if p == 0 else split(jnp.concatenate([own_rows(0), own], axis=1))
        gram = dot3(split(own.T), right)
        for q in range(p + 1):
            g2[p, q * 128:(q + 1) * 128, :] = gram[:, q * 128:(q + 1) * 128]

        @role(0)
        def _():
            go_role(functools.partial(gk_copy, p), 0)

    def g_core(p):
        @role(1)
        def _():
            gk_copy(p).wait_recv()
            rows = g_rows(p, 0, 128)
            g2[p, rows, :] = g2[p, rows, :] + gk[p, rows, :]
            start(gx_copy(p), XS, 1)

    def g_x(p):
        @role(1)
        def _():
            arrive(gx_copy(p), XS)
            rows = g_rows(p, 0)
            total = (g2[p, g_rows(p, x), :] + gx[p, 1, rows, :]) + (gx[p, 0, rows, :] + gx[p, 2, rows, :])
            gz[p, z, rows, :] = total
            start(gz_copy(p), ZS, 1)

    def g_z(p):
        @role(1)
        def _():
            arrive(gz_from(p), ZS)
            total = gz[p, 0, g_rows(p, 0), :]
            for o in range(1, ZS):
                total = total + gz[p, o, g_rows(p, 0), :]
            gt[p, g_rows(p, 0), :] = total
            start(gy_copy(p), YS, 1)

    def g_y(p):
        @role(1)
        def _():
            arrive(gy_copy(p), YS)
            rows = g_rows(p, 0)
            gf[p, g_rows(p, x), :] = (gt[p, rows, :] + gy[p, 1, rows, :]) + (gy[p, 0, rows, :] + gy[p, 2, rows, :])
            start(gx_back(p), XS, 1)

    def g_x_back(p):
        @role(1)
        def _():
            arrive(gx_back(p), XS)

    def product(p, h, step, first=False):
        rows = ds(base(h, chunk(step)), CH)
        left = split(yfull[p, rows, :].T)
        for t in range(4):
            lanes = slice(t * 256, (t + 1) * 256)
            part = dot3(left, (ahi[rows, lanes], alo[rows, lanes]))
            for q in range(2):
                out = slice((2 * t + q) * 128, (2 * t + q + 1) * 128)
                if first:
                    c2[p, out, :] = part[:, q * 128:(q + 1) * 128]
                else:
                    c2[p, out, :] += part[:, q * 128:(q + 1) * 128]

    quarter = x * 256
    piece = ds(quarter + z * 32, 32)

    def core_copy(p):
        return remote(c2.at[p], ccore.at[p], core_send.at[p, 0], core_recv.at[p, 0], row=core_peer)

    def core_back(p):
        return remote(cf.at[p], cf.at[p], core_send.at[p, 1], core_recv.at[p, 1], row=core_peer)

    def x_copy(p):
        def make(o):
            xp = lax.rem(x + o, XS)
            return remote(c2.at[p, ds(xp * 256, 256)], cx.at[p, o - 1],
                          x_send.at[p, 0, o - 1], x_recv.at[p, 0, o - 1], row=row_of(xp, z, k))
        return make

    def z_copy(p):
        def make(o):
            zp = lax.rem(z + o, ZS)
            return remote(c2.at[p, ds(quarter + zp * 32, 32)], cz.at[p, o - 1],
                          z_send.at[p, 0, o - 1], z_recv.at[p, 0, o - 1], row=row_of(x, zp, k))
        return make

    def z_back(p):
        def make(o):
            return remote(cf.at[p, piece], cf.at[p, piece], z_send.at[p, 1, o - 1], z_recv.at[p, 1, o - 1],
                          row=row_of(x, lax.rem(z + o, ZS), k))
        return make

    def x_back(p):
        def make(o):
            ref = cf.at[p, ds(quarter, 256)]
            return remote(ref, ref, x_send.at[p, 1, o - 1], x_recv.at[p, 1, o - 1],
                          row=row_of(lax.rem(x + o, XS), z, k))
        return make

    def c_send(p):
        @role(1)
        def _():
            go_role(functools.partial(core_copy, p), 1)

    def c_core(p):
        @role(0)
        def _():
            core_copy(p).wait_recv()
            c2[p] = c2[p] + ccore[p]
            start(x_copy(p), XS, 0)

    def c_x(p):
        @role(0)
        def _():
            arrive(x_copy(p), XS)
            rows = ds(quarter, 256)
            c2[p, rows, :] = (c2[p, rows, :] + cx[p, 0]) + (cx[p, 1] + cx[p, 2])
            start(z_copy(p), ZS, 0)

    def c_z(p):
        @role(0)
        def _():
            arrive(z_copy(p), ZS)
            total = c2[p, piece, :]
            for o in range(ZS - 1):
                total = total + cz[p, o]
            cf[p, piece, :] = total
            start(z_back(p), ZS, 0)

    def c_z_back(p):
        @role(0)
        def _():
            arrive(z_back(p), ZS)
            start(x_back(p), XS, 0)

    def c_x_back(p):
        @role(0)
        def _():
            arrive(x_back(p), XS)
            go_role(functools.partial(core_back, p), 0)

    def c_core_back(p):
        @role(1)
        def _():
            core_back(p).wait_recv()

    def eye():
        shape = (128, 128)
        same = lax.broadcasted_iota(jnp.int32, shape, 0) == lax.broadcasted_iota(jnp.int32, shape, 1)
        return same.astype(F32)

    def factor_start0():
        work[0, :, :128] = gf[0, 0:128, :] * INV_TOTAL
        work[0, :, 128:] = eye()

    def factor_start1():
        cross = fdot(work[0, :, 128:], gf[1, 0:128, :].T * INV_TOTAL)
        work[1, :, :128] = gf[1, 128:256, :] * INV_TOTAL - fdot(cross.T, cross)
        work[1, :, 128:] = eye()
        inv[:128, 128:] = cross

    def factor_end():
        inv0, inv1 = work[0, :, 128:], work[1, :, 128:]
        corner = -fdot(fdot(inv1, inv[:128, 128:].T), inv0)
        inv[:128, :128] = inv0
        inv[:128, 128:] = jnp.zeros_like(inv0)
        inv[128:, :128] = corner
        inv[128:, 128:] = inv1

    def inverse_copy():
        return remote(inv, inv, inv_sem.at[0], inv_sem.at[1], row=core_peer)

    def gathered(p):
        return jnp.concatenate([cf[p, t * 128:(t + 1) * 128, :] for t in range(8)], axis=1)

    def bases():
        across = split(inv[...].T)
        for i in range(8):
            rows = slice(i * CH, (i + 1) * CH)
            y = jnp.concatenate([yfull[0, rows, :], yfull[1, rows, :]], axis=1)
            bbuf[rows, :] = dot3(split(y), across)

    def gathered_first(p):
        for d in range(2):
            gather(p, d, d).wait_recv()
            go(gather_on(p, d))

    def gathered_second(p):
        for d in range(2):
            gather(p, d, 1 - d).wait_recv()

    def gathered_last(p):
        for d in range(2):
            gather_on(p, d).wait_recv()

    loads[units[0]].wait()
    for unit in units[2:]:
        loads[unit].start()
    for unit in units[:2]:
        sketch(*unit)
    pl.semaphore_wait(barrier, (YS - 1) + (XS - 1) + (KS - 1) + (ZS - 1))
    for p in range(2):
        for d in range(2):
            go(relay(p, d))
    for unit in units[2:4]:
        sketch(*unit)
    for d in range(2):
        go(direct(0, d))
    for unit in units[4:6]:
        sketch(*unit)
    pass_on(0)
    for d in range(2):
        go(direct(1, d))
    pass_on(1)
    for unit in units[6:]:
        sketch(*unit)
    own_sum(0)
    for d in range(2):
        go(gather(0, d, d))
    gram_local(0)
    product(0, 0, 0, True)
    for d in range(2):
        go(gather(0, d, 1 - d))
    product(0, 1, 0)
    g_core(0)
    own_sum(1)
    for d in range(2):
        go(gather(1, d, d))
    gram_local(1)
    g_x(0)
    g_core(1)
    product(1, 0, 0, True)
    product(1, 1, 0)
    gathered_first(0)
    for d in range(2):
        go(gather(1, d, 1 - d))
    product(0, 0, 3)
    product(0, 1, 1)
    gathered_second(0)
    product(0, 1, 3)
    product(0, 0, 1)
    g_x(1)
    g_z(0)
    gathered_last(0)
    product(0, 0, 2)
    product(0, 1, 2)
    c_send(0)
    gathered_first(1)
    c_core(0)
    g_y(0)
    product(1, 0, 3)
    product(1, 1, 1)
    gathered_second(1)
    product(1, 1, 3)
    product(1, 0, 1)
    g_z(1)
    c_x(0)
    gathered_last(1)
    product(1, 0, 2)
    product(1, 1, 2)
    c_send(1)
    g_y(1)
    g_x_back(0)

    def first():
        both = dot3(split(inv[:, :128]), split(gathered(0)))
        obuf[:128, :] = both[:128, :] * INV_ROOT
        obuf[128:, :] = both[128:, :]

    c_core(1)
    c_z(0)
    c_x(1)
    c_z_back(0)
    c_z(1)
    c_x_back(0)
    c_z_back(1)

    @role(1)
    def _():
        factor_start0()
        for i in (0, 4, 8, 12):
            eliminate(work.at[0], i)

    g_x_back(1)

    @role(1)
    def _():
        factor_start1()
        for i in (0, 4, 8, 12):
            eliminate(work.at[1], i)
        factor_end()
        go_role(inverse_copy, 1)

    @role(0)
    def _():
        inverse_copy().wait_recv()

    c_core_back(0)
    bases()
    first()
    c_x_back(1)
    c_core_back(1)
    last = dot3(split(inv[128:, 128:]), split(gathered(1)))
    obuf[128:, :] = (obuf[128:, :] + last) * INV_ROOT
    for core in range(2):
        @role(core)
        def _():
            for make in role_sends[core]:
                make().wait_send()

    for copy in sends:
        copy.wait_send()


def per_device(snapshots, tests):
    vmem, dma = pltpu.VMEM, pltpu.SemaphoreType.DMA
    any_spec = pl.BlockSpec(memory_space=pl.ANY)
    return pl.pallas_call(
        comm_kernel,
        out_shape=(vmem((ROWS, 256), F32), vmem((256, COLS), F32)),
        in_specs=[any_spec, any_spec],
        out_specs=(pl.BlockSpec(memory_space=vmem), pl.BlockSpec(memory_space=vmem)),
        scratch_shapes=[
            vmem((ROWS, COLS), F32), vmem((2, COLS, 128), F32), vmem((ROWS, COLS), BF16), vmem((ROWS, COLS), BF16),
            vmem((COLS, 256), BF16), vmem((COLS, 256), BF16), vmem((2, ROWS, 128), F32),
            vmem((2, 2, 3, CH, 128), F32), vmem((2, ROWS, 128), F32),
            vmem((2, 1024, 128), F32), vmem((2, 1024, 128), F32), vmem((2, 1024, 128), F32),
            vmem((2, 3, 256, 128), F32), vmem((2, 7, 32, 128), F32),
            vmem((2, 256, 128), F32), vmem((2, 256, 128), F32), vmem((2, 256, 128), F32), vmem((2, 3, 64, 128), F32),
            vmem((2, ZS, 64, 128), F32), vmem((2, 3, 64, 128), F32), vmem((2, 64, 128), F32),
            vmem((2, 128, 256), F32), vmem((256, 256), F32),
            dma((10,)), dma((2, 2, 3)), dma((2, 2, 3)), dma((2, 2, 3)), dma((2, 2, 3)),
            dma((2, 2)), dma((2, 2)), dma((2, 2, 3)), dma((2, 2, 3)), dma((2, 2, 7)), dma((2, 2, 7)), dma((2,)),
            dma((2,)), dma((2,)), dma((2, 2, 3)), dma((2, 2, 3)), dma((2, 7)), dma((2, 7)), dma((2, 3)), dma((2, 3))],
        compiler_params=pltpu.CompilerParams(collective_id=0, has_side_effects=True, vmem_limit_bytes=52 << 20),
    )(snapshots, tests)


def solution(mesh):
    in_specs = (P("row", "col"), P(None, "col", None))
    out_specs = (P("row", None), P(None, "col"))
    return jax.shard_map(per_device, mesh=mesh, in_specs=in_specs, out_specs=out_specs, check_vma=False)
```

```python
import functools
import math

import jax
import jax.numpy as jnp
from jax import lax
from jax.experimental import pallas as pl
from jax.experimental.pallas import tpu as pltpu
from jax.sharding import PartitionSpec as P

F32 = jnp.float32
BF16 = jnp.bfloat16
XS, ZS, KS, YS = 4, 8, 2, 4
MESH = pl.DeviceIdType.MESH
ROWS = 2048
COLS = 1024
CH = 256
TOTAL = float(ROWS * XS * ZS * KS)
INV_TOTAL = 1.0 / TOTAL
INV_ROOT = 1.0 / math.sqrt(TOTAL)


def split(value):
    high = value.astype(BF16)
    low = (value - high.astype(F32)).astype(BF16)
    return high, low


def bdot(left, right):
    return jnp.dot(left, right, preferred_element_type=F32)


def dot3(left, right):
    (lh, ll), (rh, rl) = left, right
    return bdot(lh, rh) + (bdot(ll, rh) + bdot(lh, rl))


def fdot(left, right):
    return jnp.dot(left, right, precision=lax.Precision.HIGHEST, preferred_element_type=F32)


def ds(start, size):
    return pl.ds(pl.multiple_of(start, 8), size)


def twice(value):
    return jnp.concatenate([value, value], axis=1)


def eliminate(work, first):
    row = lax.broadcasted_iota(jnp.int32, (8, 256), 0)
    count = 4
    slabs = [work[8 * (first + q):8 * (first + q) + 8, :] for q in range(count)]
    for q in range(count):
        off = 8 * (first + q)

        def spread(slab, j):
            return jnp.broadcast_to(slab[:, off + j:off + j + 1], (8, 128))

        columns = [spread(slabs[q], j) for j in range(8)]
        diag = [[jnp.broadcast_to(columns[j][i:i + 1, :], (8, 128)) for j in range(i + 1)] for i in range(8)]
        lines = [jnp.broadcast_to(slabs[q][i:i + 1, :], (8, 256)) for i in range(8)]
        below = {p: [spread(slabs[p], j) for j in range(8)] for p in range(q + 1, count)}
        out = None
        for j in range(8):
            scale = lax.rsqrt(diag[j][j])
            lines[j] = lines[j] * twice(scale)
            low = [None] * (j + 1) + [diag[i][j] * scale for i in range(j + 1, 8)]
            for i in range(j + 1, 8):
                for m in range(j + 1, i + 1):
                    diag[i][m] = diag[i][m] - low[i] * low[m]
                lines[i] = lines[i] - twice(low[i]) * lines[j]
            for p in range(q + 1, count):
                factor = below[p][j] * scale
                for m in range(j + 1, 8):
                    below[p][m] = below[p][m] - factor * low[m]
                slabs[p] = slabs[p] - twice(factor) * lines[j]
            out = lines[j] if out is None else jnp.where(row == j, lines[j], out)
        slabs[q] = out
        work[off:off + 8, :] = out
    end = 8 * (first + count)
    if end < 128:
        done = work[8 * first:end, :]
        work[end:, :] = work[end:, :] - fdot(done[:, :128].T[end:, :], done)


def comm_kernel(
    a_hbm, t_hbm, bbuf, obuf,
    abuf, tbuf, ahi, alo, th, tl, ypart, rs, yfull,
    c2, cf, ccore, cx, cz, g2, gf, gk, gx, gz, gy, gt, work, inv,
    load_sem, rs_send, rs_recv, ag_send, ag_recv,
    core_send, core_recv, x_send, x_recv, z_send, z_recv,
    inv_sem, gk_send, gk_recv, gx_send, gx_recv, gz_send, gz_recv, gy_send, gy_recv,
):
    r = lax.axis_index("row")
    c = lax.axis_index("col")
    x, z, k = r // (ZS * KS), (r // KS) % ZS, r % KS

    def row_of(xx, zz, kk):
        return xx * (ZS * KS) + zz * KS + kk

    def chunk(step):
        return lax.rem(c + step, YS)

    def base(d, j):
        return d * (YS * CH) + j * CH

    def remote(src, dst, ssem, rsem, **where):
        return pltpu.make_async_remote_copy(
            src_ref=src, dst_ref=dst, send_sem=ssem, recv_sem=rsem,
            device_id=where, device_id_type=MESH)

    sends = []
    role_sends = ([], [])

    def go(copy):
        copy.start()
        sends.append(copy)

    def go_role(make, core):
        make().start()
        role_sends[core].append(make)

    def start(make, count, core):
        for o in sorted(range(1, count), key=lambda o: -min(o, count - o)):
            go_role(functools.partial(make, o), core)

    def arrive(make, count):
        for o in range(1, count):
            make(o).wait_recv()

    def role(core):
        return pl.when(k == core)

    barrier = pltpu.get_barrier_semaphore()
    for o in (4, 3, 5, 2, 6, 1, 7):
        pl.semaphore_signal(barrier, inc=1, device_id={"row": row_of(x, lax.rem(z + o, ZS), k)}, device_id_type=MESH)
    for o in range(1, XS):
        pl.semaphore_signal(barrier, inc=1, device_id={"row": row_of(lax.rem(x + o, XS), z, k)}, device_id_type=MESH)
    pl.semaphore_signal(barrier, inc=1, device_id={"row": row_of(x, z, 1 - k)}, device_id_type=MESH)
    for o in range(1, YS):
        pl.semaphore_signal(barrier, inc=1, device_id={"col": chunk(o)}, device_id_type=MESH)

    units = [(0, 2), (1, 2), (1, 1), (0, 3), (0, 1), (1, 3), (0, 0), (1, 0)]
    t_loads = [pltpu.make_async_copy(t_hbm.at[p], tbuf.at[p], load_sem.at[8 + p]) for p in range(2)]
    loads = {}
    for i, (h, step) in enumerate(units):
        rows = ds(base(h, chunk(step)), CH)
        loads[h, step] = pltpu.make_async_copy(a_hbm.at[rows], abuf.at[rows], load_sem.at[i])
    t_loads[0].start()
    t_loads[1].start()
    for unit in units[:2]:
        loads[unit].start()
    for p in range(2):
        t_loads[p].wait()
        high, low = split(tbuf[p])
        th[:, p * 128:(p + 1) * 128] = high
        tl[:, p * 128:(p + 1) * 128] = low

    steps = (1, 3)

    def to(d):
        return chunk(steps[d])

    def relay(p, d):
        return remote(ypart.at[p, ds(base(d, chunk(2)), CH)], rs.at[p, d, 0],
                      rs_send.at[p, d, 0], rs_recv.at[p, d, 0], col=to(d))

    def direct(p, d):
        return remote(ypart.at[p, ds(base(1 - d, to(d)), CH)], rs.at[p, d, 1],
                      rs_send.at[p, d, 1], rs_recv.at[p, d, 1], col=to(d))

    def relayed(p, d):
        return remote(rs.at[p, d, 0], rs.at[p, d, 2], rs_send.at[p, d, 2], rs_recv.at[p, d, 2], col=to(d))

    def pass_on(p):
        for d in range(2):
            relay(p, d).wait_recv()
            rs[p, d, 0] = rs[p, d, 0] + ypart[p, ds(base(d, to(d)), CH), :]
            go(relayed(p, d))

    def own_sum(p):
        for h in range(2):
            direct(p, 1 - h).wait_recv()
            relayed(p, h).wait_recv()
            rows = ds(base(h, c), CH)
            yfull[p, rows, :] = (rs[p, h, 2] + rs[p, 1 - h, 1]) + ypart[p, rows, :]

    def gather(p, d, h):
        ref = yfull.at[p, ds(base(h, c), CH)]
        return remote(ref, ref, ag_send.at[p, d, h], ag_recv.at[p, d, h], col=to(d))

    def gather_on(p, d):
        ref = yfull.at[p, ds(base(d, to(1 - d)), CH)]
        return remote(ref, ref, ag_send.at[p, d, 2], ag_recv.at[p, d, 2], col=to(d))

    def sketch(h, step):
        if (h, step) != units[0]:
            loads[h, step].wait()
        rows = ds(base(h, chunk(step)), CH)
        high, low = split(abuf[rows, :])
        ahi[rows, :] = high
        alo[rows, :] = low
        part = dot3((high, low), (th[...], tl[...]))
        ypart[0, rows, :] = part[:, :128]
        ypart[1, rows, :] = part[:, 128:]

    def g_rows(p, index, size=32):
        return ds(index * (size * (p + 1)), size * (p + 1))

    core_peer = row_of(x, z, 1 - k)

    def gk_copy(p):
        return remote(g2.at[p, g_rows(p, 0, 128)], gk.at[p, g_rows(p, 0, 128)], gk_send.at[p], gk_recv.at[p], row=core_peer)

    def gx_copy(p):
        def make(o):
            xp = lax.rem(x + o, XS)
            return remote(g2.at[p, g_rows(p, xp)], gx.at[p, o - 1, g_rows(p, 0)],
                          gx_send.at[p, 0, o - 1], gx_recv.at[p, 0, o - 1], row=row_of(xp, z, k))
        return make

    def gx_back(p):
        def make(o):
            ref = gf.at[p, g_rows(p, x)]
            return remote(ref, ref, gx_send.at[p, 1, o - 1], gx_recv.at[p, 1, o - 1],
                          row=row_of(lax.rem(x + o, XS), z, k))
        return make

    def gz_copy(p):
        def make(o):
            slot = gz.at[p, z, g_rows(p, 0)]
            return remote(slot, slot, gz_send.at[p, o - 1], gz_recv.at[p, o - 1], row=row_of(x, lax.rem(z + o, ZS), k))
        return make

    def gz_from(p):
        def make(o):
            slot = gz.at[p, lax.rem(z + (ZS - o), ZS), g_rows(p, 0)]
            return remote(slot, slot, gz_send.at[p, o - 1], gz_recv.at[p, o - 1], row=row_of(x, lax.rem(z + o, ZS), k))
        return make

    def gy_copy(p):
        def make(o):
            return remote(gt.at[p, g_rows(p, 0)], gy.at[p, o - 1, g_rows(p, 0)],
                          gy_send.at[p, o - 1], gy_recv.at[p, o - 1], col=chunk(o))
        return make

    def own_rows(p):
        return jnp.concatenate([yfull[p, ds(base(h, c), CH), :] for h in range(2)], axis=0)

    def gram_local(p):
        own = own_rows(p)
        right = split(own) if p == 0 else split(jnp.concatenate([own_rows(0), own], axis=1))
        gram = dot3(split(own.T), right)
        for q in range(p + 1):
            g2[p, q * 128:(q + 1) * 128, :] = gram[:, q * 128:(q + 1) * 128]

        @role(0)
        def _():
            go_role(functools.partial(gk_copy, p), 0)

    def g_core(p):
        @role(1)
        def _():
            gk_copy(p).wait_recv()
            rows = g_rows(p, 0, 128)
            g2[p, rows, :] = g2[p, rows, :] + gk[p, rows, :]
            start(gx_copy(p), XS, 1)

    def g_x(p):
        @role(1)
        def _():
            arrive(gx_copy(p), XS)
            rows = g_rows(p, 0)
            total = (g2[p, g_rows(p, x), :] + gx[p, 1, rows, :]) + (gx[p, 0, rows, :] + gx[p, 2, rows, :])
            gz[p, z, rows, :] = total
            start(gz_copy(p), ZS, 1)

    def g_z(p):
        @role(1)
        def _():
            arrive(gz_from(p), ZS)
            total = gz[p, 0, g_rows(p, 0), :]
            for o in range(1, ZS):
                total = total + gz[p, o, g_rows(p, 0), :]
            gt[p, g_rows(p, 0), :] = total
            start(gy_copy(p), YS, 1)

    def g_y(p):
        @role(1)
        def _():
            arrive(gy_copy(p), YS)
            rows = g_rows(p, 0)
            gf[p, g_rows(p, x), :] = (gt[p, rows, :] + gy[p, 1, rows, :]) + (gy[p, 0, rows, :] + gy[p, 2, rows, :])
            start(gx_back(p), XS, 1)

    def g_x_back(p):
        @role(1)
        def _():
            arrive(gx_back(p), XS)

    def product(p, h, step, first=False):
        rows = ds(base(h, chunk(step)), CH)
        left = split(yfull[p, rows, :].T)
        for t in range(4):
            lanes = slice(t * 256, (t + 1) * 256)
            part = dot3(left, (ahi[rows, lanes], alo[rows, lanes]))
            for q in range(2):
                out = slice((2 * t + q) * 128, (2 * t + q + 1) * 128)
                if first:
                    c2[p, out, :] = part[:, q * 128:(q + 1) * 128]
                else:
                    c2[p, out, :] += part[:, q * 128:(q + 1) * 128]

    quarter = x * 256
    piece = ds(quarter + z * 32, 32)

    def core_copy(p):
        return remote(c2.at[p], ccore.at[p], core_send.at[p, 0], core_recv.at[p, 0], row=core_peer)

    def core_back(p):
        return remote(cf.at[p], cf.at[p], core_send.at[p, 1], core_recv.at[p, 1], row=core_peer)

    def x_copy(p):
        def make(o):
            xp = lax.rem(x + o, XS)
            return remote(c2.at[p, ds(xp * 256, 256)], cx.at[p, o - 1],
                          x_send.at[p, 0, o - 1], x_recv.at[p, 0, o - 1], row=row_of(xp, z, k))
        return make

    def z_copy(p):
        def make(o):
            zp = lax.rem(z + o, ZS)
            return remote(c2.at[p, ds(quarter + zp * 32, 32)], cz.at[p, o - 1],
                          z_send.at[p, 0, o - 1], z_recv.at[p, 0, o - 1], row=row_of(x, zp, k))
        return make

    def z_back(p):
        def make(o):
            return remote(cf.at[p, piece], cf.at[p, piece], z_send.at[p, 1, o - 1], z_recv.at[p, 1, o - 1],
                          row=row_of(x, lax.rem(z + o, ZS), k))
        return make

    def x_back(p):
        def make(o):
            ref = cf.at[p, ds(quarter, 256)]
            return remote(ref, ref, x_send.at[p, 1, o - 1], x_recv.at[p, 1, o - 1],
                          row=row_of(lax.rem(x + o, XS), z, k))
        return make

    def c_send(p):
        @role(1)
        def _():
            go_role(functools.partial(core_copy, p), 1)

    def c_core(p):
        @role(0)
        def _():
            core_copy(p).wait_recv()
            c2[p] = c2[p] + ccore[p]
            start(x_copy(p), XS, 0)

    def c_x(p):
        @role(0)
        def _():
            arrive(x_copy(p), XS)
            rows = ds(quarter, 256)
            c2[p, rows, :] = (c2[p, rows, :] + cx[p, 0]) + (cx[p, 1] + cx[p, 2])
            start(z_copy(p), ZS, 0)

    def c_z(p):
        @role(0)
        def _():
            arrive(z_copy(p), ZS)
            total = c2[p, piece, :]
            for o in range(ZS - 1):
                total = total + cz[p, o]
            cf[p, piece, :] = total
            start(z_back(p), ZS, 0)

    def c_z_back(p):
        @role(0)
        def _():
            arrive(z_back(p), ZS)
            start(x_back(p), XS, 0)

    def c_x_back(p):
        @role(0)
        def _():
            arrive(x_back(p), XS)
            go_role(functools.partial(core_back, p), 0)

    def c_core_back(p):
        @role(1)
        def _():
            core_back(p).wait_recv()

    def eye():
        shape = (128, 128)
        same = lax.broadcasted_iota(jnp.int32, shape, 0) == lax.broadcasted_iota(jnp.int32, shape, 1)
        return same.astype(F32)

    def factor_start0():
        work[0, :, :128] = gf[0, 0:128, :] * INV_TOTAL
        work[0, :, 128:] = eye()

    def factor_start1():
        cross = fdot(work[0, :, 128:], gf[1, 0:128, :].T * INV_TOTAL)
        work[1, :, :128] = gf[1, 128:256, :] * INV_TOTAL - fdot(cross.T, cross)
        work[1, :, 128:] = eye()
        inv[:128, 128:] = cross

    def factor_end():
        inv0, inv1 = work[0, :, 128:], work[1, :, 128:]
        corner = -fdot(fdot(inv1, inv[:128, 128:].T), inv0)
        inv[:128, :128] = inv0
        inv[:128, 128:] = jnp.zeros_like(inv0)
        inv[128:, :128] = corner
        inv[128:, 128:] = inv1

    def inverse_copy():
        return remote(inv, inv, inv_sem.at[0], inv_sem.at[1], row=core_peer)

    def gathered(p):
        return jnp.concatenate([cf[p, t * 128:(t + 1) * 128, :] for t in range(8)], axis=1)

    def bases():
        across = split(inv[...].T)
        for i in range(8):
            rows = slice(i * CH, (i + 1) * CH)
            y = jnp.concatenate([yfull[0, rows, :], yfull[1, rows, :]], axis=1)
            bbuf[rows, :] = dot3(split(y), across)

    def gathered_first(p):
        for d in range(2):
            gather(p, d, d).wait_recv()
            go(gather_on(p, d))

    def gathered_second(p):
        for d in range(2):
            gather(p, d, 1 - d).wait_recv()

    def gathered_last(p):
        for d in range(2):
            gather_on(p, d).wait_recv()

    loads[units[0]].wait()
    for unit in units[2:]:
        loads[unit].start()
    for unit in units[:2]:
        sketch(*unit)
    pl.semaphore_wait(barrier, (YS - 1) + (XS - 1) + (KS - 1) + (ZS - 1))
    for p in range(2):
        for d in range(2):
            go(relay(p, d))
    for unit in units[2:4]:
        sketch(*unit)
    for d in range(2):
        go(direct(0, d))
    for unit in units[4:6]:
        sketch(*unit)
    pass_on(0)
    for d in range(2):
        go(direct(1, d))
    pass_on(1)
    for unit in units[6:]:
        sketch(*unit)
    own_sum(0)
    for d in range(2):
        go(gather(0, d, d))
    gram_local(0)
    product(0, 0, 0, True)
    for d in range(2):
        go(gather(0, d, 1 - d))
    product(0, 1, 0)
    g_core(0)
    own_sum(1)
    for d in range(2):
        go(gather(1, d, d))
    gram_local(1)
    g_x(0)
    g_core(1)
    product(1, 0, 0, True)
    product(1, 1, 0)
    gathered_first(0)
    for d in range(2):
        go(gather(1, d, 1 - d))
    product(0, 0, 3)
    product(0, 1, 1)
    gathered_second(0)
    product(0, 1, 3)
    product(0, 0, 1)
    g_x(1)
    g_z(0)
    gathered_last(0)
    product(0, 0, 2)
    product(0, 1, 2)
    c_send(0)
    gathered_first(1)
    c_core(0)
    g_y(0)
    product(1, 0, 3)
    product(1, 1, 1)
    gathered_second(1)
    product(1, 1, 3)
    product(1, 0, 1)
    g_z(1)
    c_x(0)
    gathered_last(1)
    product(1, 0, 2)
    product(1, 1, 2)
    c_send(1)
    g_y(1)
    g_x_back(0)

    def first():
        both = dot3(split(inv[:, :128]), split(gathered(0)))
        obuf[:128, :] = both[:128, :] * INV_ROOT
        obuf[128:, :] = both[128:, :]

    c_core(1)
    c_z(0)
    c_x(1)
    c_z_back(0)
    c_z(1)
    c_x_back(0)
    c_z_back(1)

    @role(1)
    def _():
        factor_start0()
        for i in (0, 4, 8, 12):
            eliminate(work.at[0], i)

    g_x_back(1)

    @role(1)
    def _():
        factor_start1()
        for i in (0, 4, 8, 12):
            eliminate(work.at[1], i)
        factor_end()
        go_role(inverse_copy, 1)

    @role(0)
    def _():
        inverse_copy().wait_recv()

    c_core_back(0)
    bases()
    first()
    c_x_back(1)
    c_core_back(1)
    last = dot3(split(inv[128:, 128:]), split(gathered(1)))
    obuf[128:, :] = (obuf[128:, :] + last) * INV_ROOT
    for core in range(2):
        @role(core)
        def _():
            for make in role_sends[core]:
                make().wait_send()

    for copy in sends:
        copy.wait_send()


def store_kernel(basis_ref, coeff_ref, basis_hbm, coeff_hbm, sem):
    copies = []
    for src, dst, count in ((basis_ref, basis_hbm, 8), (coeff_ref, coeff_hbm, 4)):
        size = src.shape[0] // count
        for i in range(count):
            rows = pl.ds(i * size, size)
            copies.append(pltpu.make_async_copy(src.at[rows], dst.at[rows], sem.at[len(copies)]))
            copies[-1].start()
    for copy in copies:
        copy.wait()


def per_device(snapshots, tests):
    vmem, dma = pltpu.VMEM, pltpu.SemaphoreType.DMA
    any_spec = pl.BlockSpec(memory_space=pl.ANY)
    basis, coeffs = pl.pallas_call(
        comm_kernel,
        out_shape=(vmem((ROWS, 256), F32), vmem((256, COLS), F32)),
        in_specs=[any_spec, any_spec],
        out_specs=(pl.BlockSpec(memory_space=vmem), pl.BlockSpec(memory_space=vmem)),
        scratch_shapes=[
            vmem((ROWS, COLS), F32), vmem((2, COLS, 128), F32), vmem((ROWS, COLS), BF16), vmem((ROWS, COLS), BF16),
            vmem((COLS, 256), BF16), vmem((COLS, 256), BF16), vmem((2, ROWS, 128), F32),
            vmem((2, 2, 3, CH, 128), F32), vmem((2, ROWS, 128), F32),
            vmem((2, 1024, 128), F32), vmem((2, 1024, 128), F32), vmem((2, 1024, 128), F32),
            vmem((2, 3, 256, 128), F32), vmem((2, 7, 32, 128), F32),
            vmem((2, 256, 128), F32), vmem((2, 256, 128), F32), vmem((2, 256, 128), F32), vmem((2, 3, 64, 128), F32),
            vmem((2, ZS, 64, 128), F32), vmem((2, 3, 64, 128), F32), vmem((2, 64, 128), F32),
            vmem((2, 128, 256), F32), vmem((256, 256), F32),
            dma((10,)), dma((2, 2, 3)), dma((2, 2, 3)), dma((2, 2, 3)), dma((2, 2, 3)),
            dma((2, 2)), dma((2, 2)), dma((2, 2, 3)), dma((2, 2, 3)), dma((2, 2, 7)), dma((2, 2, 7)), dma((2,)),
            dma((2,)), dma((2,)), dma((2, 2, 3)), dma((2, 2, 3)), dma((2, 7)), dma((2, 7)), dma((2, 3)), dma((2, 3))],
        compiler_params=pltpu.CompilerParams(collective_id=0, has_side_effects=True, vmem_limit_bytes=52 << 20),
    )(snapshots, tests)
    return pl.pallas_call(
        store_kernel,
        out_shape=(jax.ShapeDtypeStruct((ROWS, 256), F32), jax.ShapeDtypeStruct((256, COLS), F32)),
        in_specs=[pl.BlockSpec(memory_space=vmem), pl.BlockSpec(memory_space=vmem)],
        out_specs=(any_spec, any_spec),
        scratch_shapes=[dma((12,))],
        compiler_params=pltpu.CompilerParams(vmem_limit_bytes=8 << 20),
    )(basis, coeffs)


def solution(mesh):
    in_specs = (P("row", "col"), P(None, "col", None))
    out_specs = (P("row", None), P(None, "col"))
    return jax.shard_map(per_device, mesh=mesh, in_specs=in_specs, out_specs=out_specs, check_vma=False)
```
